128 devices in a mesh: expert: 8 (over y, z_hi), dp: 16 (over x, z_lo, core).
Axes of the slice: x: 4, y: 4, z: 4 (z_hi: 2, z_lo: 2; z = z_hi * 2 + z_lo), core: 2. Of those that a mesh axis runs over, the one named last changes fastest.
Arguments:
- token_hidden: bfloat16 [16384, 2, 768], P(('expert', 'dp')), may hold values from -6 to 6
- token_grad: bfloat16 [16384, 2048], P(('expert', 'dp')), may hold values from -6 to 6
- routes: int32 [16384, 2], P(('expert', 'dp')), may hold values from 0 to 7, all different within a row; in each aligned block of 128 rows (0 to 127, 128 to 255, ...) at most 48 rows name the same one
- route_weight: float32 [16384, 2], P(('expert', 'dp')), may hold values from 0.2 to 1
- gradient_eigenbasis: bfloat16 [8, 2048, 2048], P('expert'), may hold values from -0.125 to 0.125
- basis_hidden: bfloat16 [8, 768, 768], P('expert'), may hold values from -0.21875 to 0.21875
- query_hidden: bfloat16 [8, 128, 768], P('expert', 'dp'), may hold values from -6 to 6
- query_grad: bfloat16 [8, 128, 2048], P('expert', 'dp'), may hold values from -6 to 6
- query_ids: int32 [8, 16], P('expert', 'dp'), may hold values from 0 to 7
- damping: float32 [8], P('expert'), may hold values from 0.05 to 0.5
Outputs:
- scores: float32 [16384, 2, 16], P(('expert', 'dp'))
- corrections: float32 [8, 2048, 768], P('expert', 'dp')
The draws below stay inside these ranges and needn't reach their ends.
Inputs may be any that keep to these rules, and one draw needn't show every extreme that they name: `routes`: in each device's block of 128 tokens no expert is named by more than 48 rows, and a token's 2 experts differ. `query_ids`: each id names a row of the same device's block of 8 query examples of that expert.
All inputs are finite; a program needn't handle non-finite values.
Results may differ from the reference program's by a relative error of at most 0.0052.
Values may be sent and summed in bfloat16 or wider, within the bound.
A program may use at most 64 MiB of HBM per device.

```python
import math
import jax
import jax.numpy as jnp
import numpy as np
from jax import lax

D = 2048
FF = 768
TOK_DEV = 128
TOP = 2
QROWS_DEV = 8
NQ_DEV = 1
EXPERTS = 8
CAP = 48
TOKENS = 16384
QROWS = 128
NQ = 16
N_EXPERT = 8
N_DP = 16


def plant(array, rng, least, high):
    longest = array.shape.index(max(array.shape))
    spots = []
    for shift in (0, 1):
        where = [jax.random.randint(jax.random.fold_in(rng, axis), (), 0, length) for axis, length in enumerate(array.shape)]
        where[longest] = (where[longest] + shift) % array.shape[longest]
        spots.append(tuple(where))
    return array.at[spots[0]].set(least).at[spots[1]].set(high)


def level_of(stream_key, shape, cuts, smallest, largest):
    level, own = 1.0, jax.random.fold_in(stream_key, 6)
    for dim, blocks in cuts:
        heights = jnp.exp(jax.random.uniform(jax.random.fold_in(own, dim), (blocks,), jnp.float32, smallest / len(cuts), largest / len(cuts)))
        level = level * jnp.repeat(heights, shape[dim] // blocks).reshape([-1 if axis == dim else 1 for axis in range(len(shape))])
    return level


def shared_out(key, own, number, rows, amount, top, bound, skew):
    sequence = jax.random.permutation(key, amount)
    heavy_load, common = portions_of(amount, rows * top, bound, skew, True), portions_of(amount, rows * top, bound, skew, False)
    places = jnp.arange(amount)

    def named(sizes, offset_by):
        used = int((sizes > 0).sum())
        fixed = max(1, used // 4)
        shifted = fixed + (places - fixed + offset_by * (used - fixed)) % max(1, amount - fixed)
        return jnp.zeros((amount,), jnp.int32).at[sequence[jnp.where(places < fixed, places, shifted)]].set(jnp.asarray(sizes, jnp.int32))

    sizes = jnp.where(number % 4 == 0, named(heavy_load, number // 4), named(common, number - number // 4 - 1))
    mixed = jax.random.permutation(jax.random.fold_in(own, 3), amount)
    giver, sink = mixed[0:amount // 2 * 2:2], mixed[1:amount // 2 * 2:2]
    margin = jnp.minimum(sizes[giver] - 1, bound - sizes[sink]) // 2
    margin = jnp.where((giver == sequence[0]) | (sink == sequence[0]) | (sizes[sink] == 0), 0, jnp.maximum(margin, 0))
    shifted = jax.random.randint(jax.random.fold_in(own, 4), (amount // 2,), 0, 1 << 20) % (margin + 1)
    sizes = sizes.at[giver].add(-shifted).at[sink].add(shifted)
    members = jnp.searchsorted(jnp.cumsum(sizes), jnp.arange(rows * top), side="right").astype(jnp.int32)
    grid = members.reshape(top, rows).T
    grid = grid[jax.random.permutation(jax.random.fold_in(own, 1), rows)]
    offset_by = jax.random.randint(jax.random.fold_in(own, 2), (rows, 1), 0, top)
    return jnp.take_along_axis(grid, (jnp.arange(top)[None, :] + offset_by) % top, axis=1)


def portions_of(count, total, bound, slope, full):
    portions = [(1 << 20) // math.isqrt(grade ** slope) + 1 for grade in range(1, count + 1)]
    largest = bound if full else min(bound, max(-(-total // count), total * portions[0] // sum(portions)))
    least = 1 if total - largest >= count - 1 else 0
    counts, surplus = [largest] + [least] * (count - 1), total - largest - least * (count - 1)
    while surplus > 0:
        candidates = [i for i in range(1, count) if counts[i] < largest] or [i for i in range(1, count) if counts[i] < bound]
        whole, remaining = sum([portions[i] for i in candidates]), surplus
        for i in candidates:
            extra = min(bound - counts[i], max(1, remaining * portions[i] // whole), surplus)
            counts[i] = counts[i] + extra
            surplus = surplus - extra
    return np.array(counts)


def centred(stream_key, shape, spread, limit, shards=(), held_as=jnp.bfloat16):
    loudness = level_of(stream_key, shape, shards, -0.22, 0.18) if shards else 1.0
    result = jax.random.normal(stream_key, shape, jnp.float32) * spread * loudness
    return jnp.minimum(jnp.maximum(result, -limit), limit).astype(held_as)


def setup_inputs(seed: int = 0) -> dict:
    seeds = jax.random.split(jax.random.key(seed), 11)
    token_hidden = centred(seeds[0], (TOKENS, TOP, FF), 1.0, 6.0, ((0, 128),))
    token_grad = centred(seeds[1], (TOKENS, D), 1.0, 6.0, ((0, 128),))
    routes_keys = jax.random.split(jax.random.fold_in(seeds[2], 1), TOKENS // TOK_DEV)
    routes_turns = jax.random.permutation(jax.random.fold_in(seeds[2], 3), TOKENS // TOK_DEV)
    routes = jax.vmap(lambda own, number: shared_out(jax.random.fold_in(seeds[2], 2), own, number, TOK_DEV, EXPERTS, TOP, CAP, 1))(routes_keys, routes_turns).reshape((TOKENS, TOP))
    route_weight = jnp.clip(0.2 + 0.8 * jax.random.uniform(seeds[3], (TOKENS, TOP), jnp.float32) ** level_of(seeds[3], (TOKENS, TOP), ((0, 128),), -0.2, 0.2), 0.2, 1.0)
    gradient_eigenbasis = centred(seeds[4], (EXPERTS, D, D), D ** -0.5, 0.125, ((0, 8),))
    basis_hidden = centred(seeds[5], (EXPERTS, FF, FF), FF ** -0.5, 0.21875, ((0, 8),))
    query_hidden = centred(seeds[6], (EXPERTS, QROWS, FF), 1.0, 6.0, ((0, 8), (1, 16)))
    query_grad = centred(seeds[7], (EXPERTS, QROWS, D), 1.0, 6.0, ((0, 8), (1, 16)))
    query_ids = plant(jax.random.randint(seeds[8], (EXPERTS, NQ), 0, QROWS_DEV), jax.random.fold_in(seeds[8], 1), 0, QROWS_DEV - 1).astype(jnp.int32)
    damping = jnp.clip(0.05 + 0.45 * jax.random.uniform(seeds[9], (EXPERTS,), jnp.float32) ** level_of(seeds[9], (EXPERTS,), ((0, 8),), -0.2, 0.2), 0.05, 0.5)
    return {"token_hidden": token_hidden, "token_grad": token_grad, "routes": routes, "route_weight": route_weight, "gradient_eigenbasis": gradient_eigenbasis, "basis_hidden": basis_hidden, "query_hidden": query_hidden, "query_grad": query_grad, "query_ids": query_ids, "damping": damping}


eps = 1e-06

def slot_index(routes_flat, experts, capacity):
    onehot = (routes_flat[:, None] == jnp.arange(experts, dtype=jnp.int32)[None, :]).astype(jnp.int32)
    before = jnp.cumsum(onehot, axis=0) - onehot
    return (routes_flat * capacity + lax.optimization_barrier(jnp.sum(before * onehot, axis=1))).astype(jnp.int32)

def reference(token_hidden, token_grad, routes, route_weight, gradient_eigenbasis, basis_hidden, query_hidden, query_grad, query_ids, damping):
    blocks = N_EXPERT * N_DP
    slots = jax.vmap(lambda line: slot_index(line, EXPERTS, CAP))(routes.reshape(blocks, TOK_DEV * TOP).astype(jnp.int32))
    weighted = (route_weight[:, :, None] * token_grad[:, None, :].astype(jnp.float32)).astype(jnp.bfloat16)

    def place(index, rows):
        return jnp.zeros((EXPERTS * CAP, rows.shape[-1]), jnp.bfloat16).at[index].set(rows)
    send_hidden = jax.vmap(place)(slots, token_hidden.reshape(blocks, TOK_DEV * TOP, FF))
    send_grad = jax.vmap(place)(slots, weighted.reshape(blocks, TOK_DEV * TOP, D))
    recv_hidden = jnp.transpose(send_hidden.reshape(N_EXPERT, N_DP, EXPERTS, CAP, FF), (2, 1, 0, 3, 4)).reshape(EXPERTS, N_DP, N_EXPERT * CAP, FF)
    recv_grad = jnp.transpose(send_grad.reshape(N_EXPERT, N_DP, EXPERTS, CAP, D), (2, 1, 0, 3, 4)).reshape(EXPERTS, N_DP, N_EXPERT * CAP, D)
    scale = 1.0 / (N_DP * N_EXPERT * CAP)
    root = math.sqrt(D * FF)

    def one_expert(items):
        hid_in, grad_in, rot_g, rot_h, q_hid, q_grad, ids, damp = items
        hid = jnp.einsum('rsf,fg->rsg', hid_in.astype(jnp.float32), rot_h.astype(jnp.float32)).astype(jnp.bfloat16)
        gradient_rows = jnp.einsum('rsd,de->rse', grad_in.astype(jnp.float32), rot_g.astype(jnp.float32)).astype(jnp.bfloat16)
        grad_sq = jnp.square(gradient_rows.astype(jnp.float32)).astype(jnp.bfloat16)
        hid_sq = jnp.square(hid.astype(jnp.float32)).astype(jnp.bfloat16)
        total = jnp.einsum('rsd,rsf->df', grad_sq.astype(jnp.float32), hid_sq.astype(jnp.float32)) * scale
        level = damp * (jnp.mean(total) + eps)
        inverse = (1.0 / (total + level)).astype(jnp.bfloat16)
        owner = jnp.arange(NQ, dtype=jnp.int32) // NQ_DEV
        picks = (owner * QROWS_DEV + ids).astype(jnp.int32)
        q_g = jnp.take(q_grad, picks, axis=0)
        q_h = jnp.take(q_hid, picks, axis=0)
        q_g_rot = jnp.dot(q_g, rot_g, preferred_element_type=jnp.float32).astype(jnp.bfloat16)
        q_h_rot = jnp.dot(q_h, rot_h, preferred_element_type=jnp.float32).astype(jnp.bfloat16)
        hid_wide = hid.astype(jnp.float32)
        grad_wide = gradient_rows.astype(jnp.float32)
        inverse_wide = inverse.astype(jnp.float32)

        def score_one(carry, pair):
            one_grad, one_hid = pair
            mixing = (inverse_wide * one_grad.astype(jnp.float32)[:, None] * one_hid.astype(jnp.float32)[None, :]).astype(jnp.bfloat16)
            product = jnp.einsum('rsd,df->rsf', grad_wide, mixing.astype(jnp.float32))
            return (carry, lax.optimization_barrier(jnp.sum(product * hid_wide, axis=-1)) / root)
        carry, slot_scores = lax.scan(score_one, jnp.zeros((), jnp.float32), (q_g_rot, q_h_rot))
        return (total, slot_scores)
    corrections, slot_scores = lax.map(one_expert, (recv_hidden, recv_grad, gradient_eigenbasis, basis_hidden, query_hidden, query_grad, query_ids, damping))
    grouped = jnp.transpose(slot_scores.reshape(EXPERTS, NQ, N_DP, N_EXPERT, CAP), (3, 2, 0, 4, 1)).reshape(blocks, EXPERTS * CAP, NQ)
    scores = jax.vmap(lambda table, index: jnp.take(table, index, axis=0))(grouped, slots).reshape(TOKENS, TOP, NQ)
    return (scores, corrections)
```

```python
import functools
import math

import jax
import jax.numpy as jnp
from jax import lax
from jax.experimental import pallas as pl
from jax.experimental.pallas import tpu as pltpu
from jax.sharding import Mesh
from jax.sharding import PartitionSpec as P

DP = ("dp_0", "dp_1", "dp_2")
EXPERT_DP = ("expert", "dp_0", "dp_1", "dp_2")

eps = 1e-06


def score_kernel(group, g_ref, h_ref, inv_ref, qg_ref, qh_ref, out_ref):
    rows = g_ref.shape[0]
    lane = lax.broadcasted_iota(jnp.int32, out_ref.shape, 1)
    step = pl.program_id(0)
    gq = jnp.concatenate(
        [g_ref[...] * qg_ref[k].astype(jnp.bfloat16) for k in range(group)], axis=0
    )
    product = jnp.dot(gq, inv_ref[...], preferred_element_type=jnp.float32)
    wide = h_ref[...].astype(jnp.float32)

    @pl.when(step == 0)
    def _():
        out_ref[...] = jnp.zeros_like(out_ref)

    total = out_ref[...]
    for k in range(group):
        n = step * group + k
        value = jnp.sum(product[k * rows : (k + 1) * rows] * (wide * qh_ref[k]), axis=1, keepdims=True)
        total = jnp.where(lane == n, value, total)
    out_ref[...] = total


def scored(g, h, inverse, qg, qh, group=2):
    rows = g.shape[0]
    queries = qg.shape[0]
    whole = lambda a: pl.BlockSpec(a.shape, lambda n: (0, 0), pipeline_mode=pl.Buffered(1))
    out = pl.pallas_call(
        functools.partial(score_kernel, group),
        grid=(queries // group,),
        in_specs=[whole(a) for a in (g, h, inverse)]
        + [pl.BlockSpec((group, 1, a.shape[2]), lambda n: (n, 0, 0)) for a in (qg, qh)],
        out_specs=pl.BlockSpec((rows, 128), lambda n: (0, 0)),
        out_shape=jax.ShapeDtypeStruct((rows, 128), jnp.float32),
        compiler_params=pltpu.CompilerParams(vmem_limit_bytes=50 * 1024 * 1024),
    )(g, h, inverse, qg, qh)
    return out[:, :queries]


def slot_index(routes_flat, experts, capacity):
    onehot = (routes_flat[:, None] == jnp.arange(experts, dtype=jnp.int32)[None, :]).astype(
        jnp.int32
    )
    before = jnp.cumsum(onehot, axis=0) - onehot
    return routes_flat * capacity + jnp.sum(before * onehot, axis=1)


def traded(blocks, axis):
    return lax.all_to_all(blocks, axis, split_axis=0, concat_axis=0, tiled=True)


def for_each(shard, axis):
    return traded(jnp.broadcast_to(shard, (lax.axis_size(axis), *shard.shape)), axis)


def body(
    token_hidden,
    token_grad,
    routes,
    route_weight,
    gradient_eigenbasis,
    basis_hidden,
    query_hidden,
    query_grad,
    query_ids,
    damping,
):
    experts = lax.axis_size("expert")
    replicas = lax.axis_size(DP)
    tok_rows, top, width_ff = token_hidden.shape
    width_d = token_grad.shape[1]
    capacity = tok_rows * top * 3 // (2 * experts)
    slots = slot_index(routes.reshape(-1), experts, capacity)
    weighted = (route_weight[:, :, None] * token_grad[:, None, :].astype(jnp.float32)).astype(
        jnp.bfloat16
    )
    rows = jnp.concatenate(
        (token_hidden.reshape(-1, width_ff), weighted.reshape(-1, width_d)), axis=1
    )
    chosen = (slots[None, :] == jnp.arange(experts * capacity, dtype=jnp.int32)[:, None]).astype(
        jnp.bfloat16
    )
    sent = jnp.dot(chosen, rows, preferred_element_type=jnp.float32).astype(jnp.bfloat16)
    held = traded(sent.reshape(experts, capacity, -1), "expert").reshape(experts * capacity, -1)
    rotate_h = basis_hidden[0]
    rotate_gradient = gradient_eigenbasis[0]
    picks = query_ids[0]
    query_g = jnp.take(query_grad[0], picks, axis=0)
    query_h = jnp.take(query_hidden[0], picks, axis=0)
    query_g_rot = jnp.dot(query_g, rotate_gradient, preferred_element_type=jnp.float32)
    query_h_rot = jnp.dot(query_h, rotate_h, preferred_element_type=jnp.float32)
    hid = jnp.dot(held[:, :width_ff], rotate_h, preferred_element_type=jnp.float32).astype(
        jnp.bfloat16
    )
    grad = jnp.dot(held[:, width_ff:], rotate_gradient, preferred_element_type=jnp.float32).astype(
        jnp.bfloat16
    )
    grad_sq = jnp.square(grad.astype(jnp.float32)).astype(jnp.bfloat16)
    hid_sq = jnp.square(hid.astype(jnp.float32)).astype(jnp.bfloat16)
    own_sum = jnp.sum(
        jnp.sum(grad_sq.astype(jnp.float32), axis=1) * jnp.sum(hid_sq.astype(jnp.float32), axis=1)
    )
    partial = lax.dot_general(
        grad_sq, hid_sq, (((0,), (0,)), ((), ())), preferred_element_type=jnp.float32
    ).astype(jnp.bfloat16)
    scale = 1.0 / (replicas * experts * capacity)
    chips = lax.axis_size(("dp_0", "dp_1"))
    part = width_d // replicas
    blocks = partial.reshape(chips, 2, part, width_ff).swapaxes(0, 1)
    near = traded(blocks, "dp_2").astype(jnp.float32).sum(axis=0).astype(jnp.bfloat16)
    far = traded(near, ("dp_0", "dp_1"))
    corrections = far.astype(jnp.float32).sum(axis=0) * scale

    small = jnp.concatenate(
        (query_g_rot, query_h_rot, jnp.broadcast_to(own_sum, (query_g.shape[0], 128))), axis=1
    )
    small = for_each(small, DP)
    small = small.reshape(-1, 1, small.shape[-1])
    rounded = small[:, :, : width_d + width_ff].astype(jnp.bfloat16).astype(jnp.float32)
    all_grad = rounded[:, :, :width_d]
    all_hid = rounded[:, :, width_d:]
    complete = jnp.sum(small[:: small.shape[0] // replicas, 0, -1]) * scale
    level = damping[0] * (complete / (width_d * width_ff) + eps)
    inverse = (1.0 / (corrections + level)).astype(jnp.bfloat16)
    inverse = for_each(inverse, ("dp_0", "dp_1"))
    inverse = for_each(inverse, "dp_2").swapaxes(0, 1).reshape(width_d, width_ff)
    root = math.sqrt(width_d * width_ff)
    slot_scores = scored(grad, hid, inverse, all_grad, all_hid) / root
    returned = traded(slot_scores.reshape(experts, capacity, -1), "expert")
    queries = all_grad.shape[0]
    scores = jnp.take(returned.reshape(-1, queries), slots, axis=0).reshape(tok_rows, top, queries)
    return (scores, corrections[None])


def solution(mesh):
    torus = Mesh(
        mesh.devices.reshape(mesh.shape["expert"], 4, 2, 2), ("expert", "dp_0", "dp_1", "dp_2")
    )
    placed = (
        P(EXPERT_DP, None, None),
        P(EXPERT_DP, None),
        P(EXPERT_DP, None),
        P(EXPERT_DP, None),
        P("expert", None, None),
        P("expert", None, None),
        P("expert", DP, None),
        P("expert", DP, None),
        P("expert", DP),
        P("expert"),
    )
    return jax.shard_map(
        body,
        mesh=torus,
        in_specs=placed,
        out_specs=(P(EXPERT_DP, None, None), P("expert", DP, None)),
        check_vma=False,
    )
```

```python
import functools
import math

import jax
import jax.numpy as jnp
from jax import lax
from jax.experimental import pallas as pl
from jax.experimental.pallas import tpu as pltpu
from jax.sharding import Mesh
from jax.sharding import PartitionSpec as P

DP = ("dp_0", "dp_1", "dp_2")
EXPERT_DP = ("expert", "dp_0", "dp_1", "dp_2")

eps = 1e-06


MESH = pl.DeviceIdType.MESH
CHUNK = 128


def back_kernel(
    scale,
    root,
    g_ref,
    h_ref,
    small_ref,
    slots_ref,
    damp_ref,
    out_ref,
    corr_ref,
    gsq,
    hsq,
    small,
    part,
    nearby,
    summed,
    far,
    inv,
    acc,
    ret_out,
    ret_in,
    small_s,
    small_r,
    core_s,
    core_r,
    rs_s,
    rs_r,
    ag_s,
    ag_r,
    cg_s,
    cg_r,
    ret_s,
    ret_r,
):
    e = lax.axis_index("expert")
    x = lax.axis_index("dp_0")
    z = lax.axis_index("dp_1")
    k = lax.axis_index("dp_2")
    xz = x * 2 + z
    chips = part.shape[2]
    experts = ret_out.shape[0]
    capacity = ret_out.shape[1]
    rows, width_d = g_ref.shape
    width_ff = h_ref.shape[1]
    chunks = width_ff // CHUNK
    bf16, f32 = jnp.bfloat16, jnp.float32

    def dp_id(index):
        return {"dp_0": index // 4, "dp_1": lax.rem(index // 2, 2), "dp_2": lax.rem(index, 2)}

    def chip_id(index):
        return {"dp_0": index // 2, "dp_1": lax.rem(index, 2)}

    me = xz * 2 + k
    barrier = pltpu.get_barrier_semaphore()

    def greet_dp(d, _):
        pl.semaphore_signal(
            barrier, 1, device_id=dp_id(lax.rem(me + d, 2 * chips)), device_id_type=MESH
        )
        return 0

    def greet_expert(d, _):
        pl.semaphore_signal(
            barrier, 1, device_id={"expert": lax.rem(e + d, experts)}, device_id_type=MESH
        )
        return 0

    lax.fori_loop(1, 2 * chips, greet_dp, 0)
    lax.fori_loop(1, experts, greet_expert, 0)

    gsq[...] = jnp.square(g_ref[...].astype(f32)).astype(bf16)
    hsq[...] = jnp.square(h_ref[...].astype(f32)).astype(bf16)
    acc[...] = jnp.zeros_like(acc)
    pl.semaphore_wait(barrier, 2 * chips - 1 + experts - 1)

    def core_copy(c):
        return pltpu.make_async_remote_copy(
            part.at[c, 1 - k],
            nearby.at[c],
            core_s.at[c],
            core_r.at[c],
            device_id={"dp_2": 1 - k},
            device_id_type=MESH,
        )

    def rs_copy(c, d):
        to = lax.rem(xz + d, chips)
        return pltpu.make_async_remote_copy(
            summed.at[c, to],
            far.at[c, d],
            rs_s.at[c, d],
            rs_r.at[c, d],
            device_id=chip_id(to),
            device_id_type=MESH,
        )

    def ag_copy(c, d):
        to = lax.rem(xz + d, chips)
        return pltpu.make_async_remote_copy(
            inv.at[c, k, xz],
            inv.at[c, k, xz],
            ag_s.at[c, d],
            ag_r.at[c, d],
            device_id=chip_id(to),
            device_id_type=MESH,
        )

    def ag_arrival(c, d):
        origin = lax.rem(xz + chips - d, chips)
        return pltpu.make_async_remote_copy(
            inv.at[c, k, origin],
            inv.at[c, k, origin],
            ag_s.at[c, d],
            ag_r.at[c, d],
            device_id=chip_id(origin),
            device_id_type=MESH,
        )

    def cg_copy(c, side):
        return pltpu.make_async_remote_copy(
            inv.at[c, side],
            inv.at[c, side],
            cg_s.at[c],
            cg_r.at[c],
            device_id={"dp_2": 1 - k},
            device_id_type=MESH,
        )

    def small_copy(d, slot):
        return pltpu.make_async_remote_copy(
            small.at[me],
            small.at[slot],
            small_s.at[d],
            small_r.at[d],
            device_id=dp_id(lax.rem(me + d, 2 * chips)),
            device_id_type=MESH,
        )

    def each(first, last, act):
        def once(d, _):
            act(d)
            return 0

        lax.fori_loop(first, last, once, 0)

    for pair in range(chunks // 2):
        both = lax.dot_general(
            hsq[:, pair * 2 * CHUNK : (pair + 1) * 2 * CHUNK],
            gsq[...],
            (((0,), (0,)), ((), ())),
            preferred_element_type=f32,
        ).astype(bf16)
        for half in range(2):
            for q in range(2 * chips):
                part[2 * pair + half, q % 2, q // 2] = both[
                    half * CHUNK : (half + 1) * CHUNK, q * CHUNK : (q + 1) * CHUNK
                ]
        for half in range(2):
            core_copy(2 * pair + half).start()

    row_g = jnp.sum(gsq[...].astype(f32), axis=1, keepdims=True)
    row_h = jnp.sum(hsq[...].astype(f32), axis=1, keepdims=True)
    own_sum = jnp.sum(row_g * row_h, axis=0, keepdims=True)
    place = lax.broadcasted_iota(jnp.int32, small_ref.shape, 0)
    small[me] = jnp.where(place == 22, jnp.broadcast_to(own_sum, small_ref.shape), small_ref[...])
    each(1, 2 * chips, lambda d: small_copy(d, me).start())

    def stage_one(c):
        core_copy(c).wait()
        summed[c] = (part[c, k].astype(f32) + nearby[c].astype(f32)).astype(bf16)
        each(1, chips, lambda d: rs_copy(c, d).start())

    def stage_two(c, level):
        each(1, chips, lambda d: rs_copy(c, d).wait_recv())
        total = summed[c, xz].astype(f32)
        for d in range(1, chips):
            total = total + far[c, d].astype(f32)
        block = total.T * scale
        corr_ref[:, c * CHUNK : (c + 1) * CHUNK] = block
        inv[c, k, xz] = (1.0 / (block + level)).astype(bf16)
        each(1, chips, lambda d: ag_copy(c, d).start())

    def stage_three(c):
        each(1, chips, lambda d: ag_arrival(c, d).wait_recv())
        cg_copy(c, k).start()

    def ready(c):
        cg_copy(c, 1 - k).wait_recv()

    lane = lax.broadcasted_iota(jnp.int32, acc.shape, 1)
    group = 4

    def score(pair, first, last):
        def step(t, _):
            parts = []
            for j in range(group):
                n = t * group + j
                pieces = []
                for q in range(2 * chips):
                    d = (q % chips) * 2 + q // chips
                    pieces.append(
                        g_ref[:, d * CHUNK : (d + 1) * CHUNK]
                        * small[n, d : d + 1, :].astype(bf16)
                    )
                parts.append(jnp.concatenate(pieces, axis=1))
            scaled = jnp.concatenate(parts, axis=0)
            weights = jnp.concatenate(
                [inv[2 * pair + half].reshape(width_d, CHUNK) for half in range(2)], axis=1
            )
            product = jnp.dot(scaled, weights, preferred_element_type=f32)
            total = acc[...]
            for j in range(group):
                n = t * group + j
                value = None
                for half in range(2):
                    c = 2 * pair + half
                    term = product[
                        j * rows : (j + 1) * rows, half * CHUNK : (half + 1) * CHUNK
                    ] * (
                        h_ref[:, c * CHUNK : (c + 1) * CHUNK].astype(f32)
                        * small[n, 16 + c : 17 + c, :]
                    )
                    value = term if value is None else value + term
                total = total + jnp.where(
                    lane == n, jnp.sum(value, axis=1, keepdims=True), 0.0
                )
            acc[...] = total
            return 0

        lax.fori_loop(first, last, step, 0)

    stage_one(0)
    stage_one(1)

    def small_arrival(d):
        small_copy(d, lax.rem(me + 2 * chips - d, 2 * chips)).wait_recv()

    each(1, 2 * chips, small_arrival)
    complete = small[0, 22:23, :]
    for n in range(1, 2 * chips):
        complete = complete + small[n, 22:23, :]
    level = damp_ref[...] * (complete * (scale / (width_d * width_ff)) + eps)

    stage_two(0, level)
    stage_one(2)
    stage_two(1, level)
    stage_one(3)
    stage_three(0)
    stage_two(2, level)
    stage_one(4)
    stage_three(1)
    stage_two(3, level)
    stage_one(5)
    ready(0)
    ready(1)
    score(0, 0, 2)
    stage_three(2)
    score(0, 2, 3)
    stage_two(4, level)
    score(0, 3, 4)
    stage_three(3)
    stage_two(5, level)
    ready(2)
    ready(3)
    score(1, 0, 2)
    stage_three(4)
    score(1, 2, 4)
    stage_three(5)
    ready(4)
    ready(5)
    score(2, 0, 4)

    ret_out[...] = (acc[...] / root).reshape(ret_out.shape)

    def ret_copy(d, slot):
        to = lax.rem(e + d, experts)
        return pltpu.make_async_remote_copy(
            ret_out.at[to],
            ret_in.at[slot],
            ret_s.at[d],
            ret_r.at[d],
            device_id={"expert": to},
            device_id_type=MESH,
        )

    each(1, experts, lambda d: ret_copy(d, e).start())
    ret_in[e] = ret_out[e]
    chosen = (
        slots_ref[...]
        == lax.broadcasted_iota(jnp.int32, (out_ref.shape[0], experts * capacity), 1)
    ).astype(f32)
    each(1, experts, lambda d: ret_copy(d, lax.rem(e + experts - d, experts)).wait_recv())
    out_ref[...] = jnp.dot(
        chosen,
        ret_in[...].reshape(experts * capacity, -1),
        preferred_element_type=f32,
        precision=lax.Precision.HIGHEST,
    )
    for c in range(chunks):
        each(1, chips, lambda d: rs_copy(c, d).wait_send())
        each(1, chips, lambda d: ag_copy(c, d).wait_send())
        cg_copy(c, k).wait_send()
    each(1, 2 * chips, lambda d: small_copy(d, me).wait_send())
    each(1, experts, lambda d: ret_copy(d, e).wait_send())


def back_half(grad, hid, small, slots, damp, experts, capacity, replicas):
    rows, width_d = grad.shape
    width_ff = hid.shape[1]
    chips = replicas // 2
    chunks = width_ff // CHUNK
    bf16, f32 = jnp.bfloat16, jnp.float32
    block = width_d // replicas
    dma = pltpu.SemaphoreType.DMA
    vmem = pl.BlockSpec(memory_space=pltpu.VMEM)
    return pl.pallas_call(
        functools.partial(
            back_kernel, 1.0 / (replicas * experts * capacity), math.sqrt(width_d * width_ff)
        ),
        out_shape=(
            jax.ShapeDtypeStruct((slots.shape[0], 128), f32),
            jax.ShapeDtypeStruct((block, width_ff), f32),
        ),
        in_specs=[vmem] * 5,
        out_specs=(vmem, vmem),
        scratch_shapes=[
            pltpu.VMEM((rows, width_d), bf16),
            pltpu.VMEM((rows, width_ff), bf16),
            pltpu.VMEM((replicas, *small.shape), f32),
            pltpu.VMEM((chunks, 2, chips, CHUNK, block), bf16),
            pltpu.VMEM((chunks, chips, CHUNK, block), bf16),
            pltpu.VMEM((chunks, chips, CHUNK, block), bf16),
            pltpu.VMEM((chunks, chips, CHUNK, block), bf16),
            pltpu.VMEM((chunks, 2, chips, block, CHUNK), bf16),
            pltpu.VMEM((rows, 128), f32),
            pltpu.VMEM((experts, capacity, 128), f32),
            pltpu.VMEM((experts, capacity, 128), f32),
            dma((replicas,)),
            dma((replicas,)),
            dma((chunks,)),
            dma((chunks,)),
            dma((chunks, chips)),
            dma((chunks, chips)),
            dma((chunks, chips)),
            dma((chunks, chips)),
            dma((chunks,)),
            dma((chunks,)),
            dma((experts,)),
            dma((experts,)),
        ],
        compiler_params=pltpu.CompilerParams(
            collective_id=0, has_side_effects=True, vmem_limit_bytes=60 * 1024 * 1024
        ),
    )(grad, hid, small, slots, damp)


def slot_index(routes_flat, experts, capacity):
    onehot = (routes_flat[:, None] == jnp.arange(experts, dtype=jnp.int32)[None, :]).astype(
        jnp.int32
    )
    before = jnp.cumsum(onehot, axis=0) - onehot
    return routes_flat * capacity + jnp.sum(before * onehot, axis=1)


def traded(blocks, axis):
    return lax.all_to_all(blocks, axis, split_axis=0, concat_axis=0, tiled=True)


def body(
    token_hidden,
    token_grad,
    routes,
    route_weight,
    gradient_eigenbasis,
    basis_hidden,
    query_hidden,
    query_grad,
    query_ids,
    damping,
):
    experts = lax.axis_size("expert")
    replicas = lax.axis_size(DP)
    tok_rows, top, width_ff = token_hidden.shape
    width_d = token_grad.shape[1]
    capacity = tok_rows * top * 3 // (2 * experts)
    slots = slot_index(routes.reshape(-1), experts, capacity)
    weighted = (route_weight[:, :, None] * token_grad[:, None, :].astype(jnp.float32)).astype(
        jnp.bfloat16
    )
    rows = jnp.concatenate(
        (token_hidden.reshape(-1, width_ff), weighted.reshape(-1, width_d)), axis=1
    )
    chosen = (slots[None, :] == jnp.arange(experts * capacity, dtype=jnp.int32)[:, None]).astype(
        jnp.bfloat16
    )
    sent = jnp.dot(chosen, rows, preferred_element_type=jnp.float32).astype(jnp.bfloat16)
    held = traded(sent.reshape(experts, capacity, -1), "expert").reshape(experts * capacity, -1)
    rotate_h = basis_hidden[0]
    rotate_gradient = gradient_eigenbasis[0]
    picks = query_ids[0]
    query_g = jnp.take(query_grad[0], picks, axis=0)
    query_h = jnp.take(query_hidden[0], picks, axis=0)
    query_g_rot = jnp.dot(query_g, rotate_gradient, preferred_element_type=jnp.float32)
    query_h_rot = jnp.dot(query_h, rotate_h, preferred_element_type=jnp.float32)
    hid = jnp.dot(held[:, :width_ff], rotate_h, preferred_element_type=jnp.float32).astype(
        jnp.bfloat16
    )
    grad = jnp.dot(held[:, width_ff:], rotate_gradient, preferred_element_type=jnp.float32).astype(
        jnp.bfloat16
    )
    small = jnp.concatenate(
        (
            query_g_rot.astype(jnp.bfloat16).astype(jnp.float32).reshape(-1, 128),
            query_h_rot.astype(jnp.bfloat16).astype(jnp.float32).reshape(-1, 128),
            jnp.zeros((2, 128), jnp.float32),
        ),
        axis=0,
    )
    damp = jnp.broadcast_to(damping[:, None], (1, 128))
    picked, corrections = back_half(
        grad, hid, small, slots[:, None], damp, experts, capacity, replicas
    )
    scores = picked[:, :replicas].reshape(tok_rows, top, replicas)
    return (scores, corrections[None])


def solution(mesh):
    torus = Mesh(
        mesh.devices.reshape(mesh.shape["expert"], 4, 2, 2), ("expert", "dp_0", "dp_1", "dp_2")
    )
    placed = (
        P(EXPERT_DP, None, None),
        P(EXPERT_DP, None),
        P(EXPERT_DP, None),
        P(EXPERT_DP, None),
        P("expert", None, None),
        P("expert", None, None),
        P("expert", DP, None),
        P("expert", DP, None),
        P("expert", DP),
        P("expert"),
    )
    return jax.shard_map(
        body,
        mesh=torus,
        in_specs=placed,
        out_specs=(P(EXPERT_DP, None, None), P("expert", DP, None)),
        check_vma=False,
    )
```

```python
import functools
import math

import jax
import jax.numpy as jnp
from jax import lax
from jax.experimental import pallas as pl
from jax.experimental.pallas import tpu as pltpu
from jax.sharding import Mesh
from jax.sharding import PartitionSpec as P

DP = ("dp_0", "dp_1", "dp_2")
EXPERT_DP = ("expert", "dp_0", "dp_1", "dp_2")

eps = 1e-06


MESH = pl.DeviceIdType.MESH
CHUNK = 128


def back_kernel(
    scale,
    root,
    routes_ref,
    weight_ref,
    hidden_ref,
    grad_ref,
    basis_g_ref,
    basis_h_ref,
    query_g_ref,
    query_h_ref,
    ids_ref,
    damp_ref,
    out_ref,
    corr_ref,
    basis_g,
    basis_h,
    send_g,
    send_h,
    held_g,
    held_h,
    g_ref,
    h_ref,
    gsq,
    hsq,
    small,
    part,
    nearby,
    summed,
    far,
    inv,
    acc,
    ret_out,
    ret_in,
    basis_sem,
    dg_s,
    dg_r,
    dh_s,
    dh_r,
    small_s,
    small_r,
    core_s,
    core_r,
    rs_s,
    rs_r,
    ag_s,
    ag_r,
    cg_s,
    cg_r,
    ret_s,
    ret_r,
):
    e = lax.axis_index("expert")
    x = lax.axis_index("dp_0")
    z = lax.axis_index("dp_1")
    k = lax.axis_index("dp_2")
    xz = x * 2 + z
    chips = part.shape[2]
    experts = ret_out.shape[0]
    capacity = ret_out.shape[1]
    rows, width_d = g_ref.shape
    width_ff = h_ref.shape[1]
    chunks = width_ff // CHUNK
    bf16, f32 = jnp.bfloat16, jnp.float32

    def dp_id(index):
        return {"dp_0": index // 4, "dp_1": lax.rem(index // 2, 2), "dp_2": lax.rem(index, 2)}

    def chip_id(index):
        return {"dp_0": index // 2, "dp_1": lax.rem(index, 2)}

    me = xz * 2 + k
    barrier = pltpu.get_barrier_semaphore()

    def greet_dp(d, _):
        pl.semaphore_signal(
            barrier, 1, device_id=dp_id(lax.rem(me + d, 2 * chips)), device_id_type=MESH
        )
        return 0

    def greet_expert(d, _):
        pl.semaphore_signal(
            barrier, 1, device_id={"expert": lax.rem(e + d, experts)}, device_id_type=MESH
        )
        return 0

    lax.fori_loop(1, 2 * chips, greet_dp, 0)
    lax.fori_loop(1, experts, greet_expert, 0)
    load_g = pltpu.make_async_copy(basis_g_ref, basis_g, basis_sem.at[0])
    load_h = pltpu.make_async_copy(basis_h_ref, basis_h, basis_sem.at[1])
    load_g.start()
    load_h.start()

    def each(first, last, act):
        def once(d, _):
            act(d)
            return 0

        lax.fori_loop(first, last, once, 0)

    tokens = grad_ref.shape[0]
    top = routes_ref.shape[1]
    sent = tokens * top
    named = jnp.concatenate([routes_ref[:, j : j + 1] for j in range(top)], axis=0)
    onehot = (named == lax.broadcasted_iota(jnp.int32, (sent, 128), 1)).astype(f32).astype(bf16)

    def order_of(axis):
        index = lax.broadcasted_iota(jnp.int32, (sent, sent), axis)
        return jnp.where(index < tokens, index * top, (index - tokens) * top + 1)

    lower = (order_of(1) < order_of(0)).astype(f32).astype(bf16)
    before = jnp.dot(lower, onehot, preferred_element_type=f32)
    within = jnp.sum(before * onehot.astype(f32), axis=1, keepdims=True).astype(jnp.int32)
    slots = named * capacity + within
    chosen = (slots == lax.broadcasted_iota(jnp.int32, (sent, experts * capacity), 1)).astype(f32)
    picked = chosen.T.astype(bf16)
    token_grad = grad_ref[...].astype(f32)
    weighted = jnp.concatenate(
        [(weight_ref[:, j : j + 1] * token_grad).astype(bf16) for j in range(top)], axis=0
    )
    send_g[...] = (
        jnp.dot(picked, weighted, preferred_element_type=f32).astype(bf16).reshape(send_g.shape)
    )

    def dispatch_copy(source, target, ssem, rsem, d):
        to = lax.rem(e + d, experts)
        return pltpu.make_async_remote_copy(
            source.at[to],
            target.at[d],
            ssem.at[d],
            rsem.at[d],
            device_id={"expert": to},
            device_id_type=MESH,
        )

    def dg_copy(d):
        return dispatch_copy(send_g, held_g, dg_s, dg_r, d)

    def dh_copy(d):
        return dispatch_copy(send_h, held_h, dh_s, dh_r, d)

    pl.semaphore_wait(barrier, 2 * chips - 1 + experts - 1)
    each(1, experts, lambda d: dg_copy(d).start())
    send_h[...] = (
        jnp.dot(picked, hidden_ref[...], preferred_element_type=f32)
        .astype(bf16)
        .reshape(send_h.shape)
    )
    each(1, experts, lambda d: dh_copy(d).start())
    acc[...] = jnp.zeros_like(acc)

    def rotate(value, basis, rotated, squared, first):
        turned = jnp.dot(value, basis[...], preferred_element_type=f32).astype(bf16)
        count = value.shape[0]
        rotated[first : first + count, :] = turned
        squared[first : first + count, :] = jnp.square(turned.astype(f32)).astype(bf16)

    load_h.wait()
    load_g.wait()
    rotate(send_g[e], basis_g, g_ref, gsq, 0)
    query_row = lax.broadcasted_iota(jnp.int32, (query_g_ref.shape[0], 1), 0) == ids_ref[0, 0]

    def query(ref, basis):
        turned = jnp.dot(ref[...], basis[...], preferred_element_type=f32)
        one = jnp.sum(jnp.where(query_row, turned, 0.0), axis=0, keepdims=True)
        return one.astype(bf16).astype(f32)

    query_g = query(query_g_ref, basis_g)
    query_h = query(query_h_ref, basis_h)
    for first, last in ((1, experts // 2), (experts // 2, experts)):
        each(first, last, lambda d: dg_copy(d).wait_recv())
        rotate(
            held_g[first:last].reshape((last - first) * capacity, width_d),
            basis_g,
            g_ref,
            gsq,
            first * capacity,
        )
    each(1, experts, lambda d: dh_copy(d).wait_recv())
    rotate(
        jnp.concatenate(
            [send_h[e], held_h[1:experts].reshape((experts - 1) * capacity, width_ff)], axis=0
        ),
        basis_h,
        h_ref,
        hsq,
        0,
    )

    def core_copy(c):
        return pltpu.make_async_remote_copy(
            part.at[c, 1 - k],
            nearby.at[c],
            core_s.at[c],
            core_r.at[c],
            device_id={"dp_2": 1 - k},
            device_id_type=MESH,
        )

    def rs_copy(c, d):
        to = lax.rem(xz + d, chips)
        return pltpu.make_async_remote_copy(
            summed.at[c, to],
            far.at[c, d],
            rs_s.at[c, d],
            rs_r.at[c, d],
            device_id=chip_id(to),
            device_id_type=MESH,
        )

    def ag_copy(c, d):
        to = lax.rem(xz + d, chips)
        return pltpu.make_async_remote_copy(
            inv.at[c, k, xz],
            inv.at[c, k, xz],
            ag_s.at[c, d],
            ag_r.at[c, d],
            device_id=chip_id(to),
            device_id_type=MESH,
        )

    def ag_arrival(c, d):
        origin = lax.rem(xz + chips - d, chips)
        return pltpu.make_async_remote_copy(
            inv.at[c, k, origin],
            inv.at[c, k, origin],
            ag_s.at[c, d],
            ag_r.at[c, d],
            device_id=chip_id(origin),
            device_id_type=MESH,
        )

    def cg_copy(c, side):
        return pltpu.make_async_remote_copy(
            inv.at[c, side],
            inv.at[c, side],
            cg_s.at[c],
            cg_r.at[c],
            device_id={"dp_2": 1 - k},
            device_id_type=MESH,
        )

    def small_copy(d, slot):
        return pltpu.make_async_remote_copy(
            small.at[me],
            small.at[slot],
            small_s.at[d],
            small_r.at[d],
            device_id=dp_id(lax.rem(me + d, 2 * chips)),
            device_id_type=MESH,
        )

    for pair in range(chunks // 2):
        both = lax.dot_general(
            hsq[:, pair * 2 * CHUNK : (pair + 1) * 2 * CHUNK],
            gsq[...],
            (((0,), (0,)), ((), ())),
            preferred_element_type=f32,
        ).astype(bf16)
        for half in range(2):
            for q in range(2 * chips):
                part[2 * pair + half, q % 2, q // 2] = both[
                    half * CHUNK : (half + 1) * CHUNK, q * CHUNK : (q + 1) * CHUNK
                ]
        for half in range(2):
            core_copy(2 * pair + half).start()

    row_g = jnp.sum(gsq[...].astype(f32), axis=1, keepdims=True)
    row_h = jnp.sum(hsq[...].astype(f32), axis=1, keepdims=True)
    own_sum = jnp.sum(row_g * row_h, axis=0, keepdims=True)
    for j in range(width_d // 128):
        small[me, j : j + 1, :] = query_g[:, j * 128 : (j + 1) * 128]
    for j in range(width_ff // 128):
        small[me, 16 + j : 17 + j, :] = query_h[:, j * 128 : (j + 1) * 128]
    small[me, 22:24, :] = jnp.broadcast_to(own_sum, (2, 128))
    each(1, 2 * chips, lambda d: small_copy(d, me).start())

    def stage_one(c):
        core_copy(c).wait()
        summed[c] = (part[c, k].astype(f32) + nearby[c].astype(f32)).astype(bf16)
        each(1, chips, lambda d: rs_copy(c, d).start())

    def stage_two(c, level):
        each(1, chips, lambda d: rs_copy(c, d).wait_recv())
        total = summed[c, xz].astype(f32)
        for d in range(1, chips):
            total = total + far[c, d].astype(f32)
        block = total.T * scale
        corr_ref[:, c * CHUNK : (c + 1) * CHUNK] = block
        inv[c, k, xz] = (1.0 / (block + level)).astype(bf16)
        each(1, chips, lambda d: ag_copy(c, d).start())

    def stage_three(c):
        each(1, chips, lambda d: ag_arrival(c, d).wait_recv())
        cg_copy(c, k).start()

    def ready(c):
        cg_copy(c, 1 - k).wait_recv()

    lane = lax.broadcasted_iota(jnp.int32, acc.shape, 1)
    group = 4

    def score(pair, first, last):
        def step(t, _):
            parts = []
            for j in range(group):
                n = t * group + j
                pieces = []
                for q in range(2 * chips):
                    d = (q % chips) * 2 + q // chips
                    pieces.append(
                        g_ref[:, d * CHUNK : (d + 1) * CHUNK]
                        * small[n, d : d + 1, :].astype(bf16)
                    )
                parts.append(jnp.concatenate(pieces, axis=1))
            scaled = jnp.concatenate(parts, axis=0)
            weights = jnp.concatenate(
                [inv[2 * pair + half].reshape(width_d, CHUNK) for half in range(2)], axis=1
            )
            product = jnp.dot(scaled, weights, preferred_element_type=f32)
            total = acc[...]
            for j in range(group):
                n = t * group + j
                value = None
                for half in range(2):
                    c = 2 * pair + half
                    term = product[
                        j * rows : (j + 1) * rows, half * CHUNK : (half + 1) * CHUNK
                    ] * (
                        h_ref[:, c * CHUNK : (c + 1) * CHUNK].astype(f32)
                        * small[n, 16 + c : 17 + c, :]
                    )
                    value = term if value is None else value + term
                total = total + jnp.where(
                    lane == n, jnp.sum(value, axis=1, keepdims=True), 0.0
                )
            acc[...] = total
            return 0

        lax.fori_loop(first, last, step, 0)

    stage_one(0)
    stage_one(1)

    def small_arrival(d):
        small_copy(d, lax.rem(me + 2 * chips - d, 2 * chips)).wait_recv()

    each(1, 2 * chips, small_arrival)
    complete = small[0, 22:23, :]
    for n in range(1, 2 * chips):
        complete = complete + small[n, 22:23, :]
    level = damp_ref[...] * (complete * (scale / (width_d * width_ff)) + eps)

    stage_two(0, level)
    stage_one(2)
    stage_two(1, level)
    stage_one(3)
    stage_three(0)
    stage_two(2, level)
    stage_one(4)
    stage_three(1)
    stage_two(3, level)
    stage_one(5)
    ready(0)
    ready(1)
    score(0, 0, 2)
    stage_three(2)
    score(0, 2, 3)
    stage_two(4, level)
    score(0, 3, 4)
    stage_three(3)
    stage_two(5, level)
    ready(2)
    ready(3)
    score(1, 0, 2)
    stage_three(4)
    score(1, 2, 4)
    stage_three(5)
    ready(4)
    ready(5)
    score(2, 0, 4)

    ret_out[...] = (acc[...] / root).reshape(ret_out.shape)

    def ret_copy(d, slot):
        return pltpu.make_async_remote_copy(
            ret_out.at[d],
            ret_in.at[slot],
            ret_s.at[d],
            ret_r.at[d],
            device_id={"expert": lax.rem(e + experts - d, experts)},
            device_id_type=MESH,
        )

    each(1, experts, lambda d: ret_copy(d, e).start())
    ret_in[e] = ret_out[0]
    each(1, experts, lambda d: ret_copy(d, lax.rem(e + d, experts)).wait_recv())
    out_ref[...] = jnp.dot(
        chosen,
        ret_in[...].reshape(experts * capacity, -1),
        preferred_element_type=f32,
        precision=lax.Precision.HIGHEST,
    )
    for c in range(chunks):
        each(1, chips, lambda d: rs_copy(c, d).wait_send())
        each(1, chips, lambda d: ag_copy(c, d).wait_send())
        cg_copy(c, k).wait_send()
    each(1, 2 * chips, lambda d: small_copy(d, me).wait_send())
    each(1, experts, lambda d: ret_copy(d, e).wait_send())
    each(1, experts, lambda d: dg_copy(d).wait_send())
    each(1, experts, lambda d: dh_copy(d).wait_send())


def body(
    token_hidden,
    token_grad,
    routes,
    route_weight,
    gradient_eigenbasis,
    basis_hidden,
    query_hidden,
    query_grad,
    query_ids,
    damping,
):
    experts = lax.axis_size("expert")
    replicas = lax.axis_size(DP)
    tokens, top, width_ff = token_hidden.shape
    width_d = token_grad.shape[1]
    capacity = tokens * top * 3 // (2 * experts)
    rows = experts * capacity
    chips = replicas // 2
    chunks = width_ff // CHUNK
    bf16, f32 = jnp.bfloat16, jnp.float32
    block = width_d // replicas
    dma = pltpu.SemaphoreType.DMA
    vmem = pl.BlockSpec(memory_space=pltpu.VMEM)
    anywhere = pl.BlockSpec(memory_space=pl.ANY)
    smem = pl.BlockSpec(memory_space=pltpu.SMEM)
    picked, corrections = pl.pallas_call(
        functools.partial(
            back_kernel, 1.0 / (replicas * experts * capacity), math.sqrt(width_d * width_ff)
        ),
        out_shape=(
            jax.ShapeDtypeStruct((tokens * top, 128), f32),
            jax.ShapeDtypeStruct((block, width_ff), f32),
        ),
        in_specs=[vmem] * 4 + [anywhere] * 2 + [vmem] * 2 + [smem, vmem],
        out_specs=(vmem, vmem),
        scratch_shapes=[
            pltpu.VMEM((width_d, width_d), bf16),
            pltpu.VMEM((width_ff, width_ff), bf16),
            pltpu.VMEM((experts, capacity, width_d), bf16),
            pltpu.VMEM((experts, capacity, width_ff), bf16),
            pltpu.VMEM((experts, capacity, width_d), bf16),
            pltpu.VMEM((experts, capacity, width_ff), bf16),
            pltpu.VMEM((rows, width_d), bf16),
            pltpu.VMEM((rows, width_ff), bf16),
            pltpu.VMEM((rows, width_d), bf16),
            pltpu.VMEM((rows, width_ff), bf16),
            pltpu.VMEM((replicas, 24, 128), f32),
            pltpu.VMEM((chunks, 2, chips, CHUNK, block), bf16),
            pltpu.VMEM((chunks, chips, CHUNK, block), bf16),
            pltpu.VMEM((chunks, chips, CHUNK, block), bf16),
            pltpu.VMEM((chunks, chips, CHUNK, block), bf16),
            pltpu.VMEM((chunks, 2, chips, block, CHUNK), bf16),
            pltpu.VMEM((rows, 128), f32),
            pltpu.VMEM((experts, capacity, 128), f32),
            pltpu.VMEM((experts, capacity, 128), f32),
            dma((2,)),
            dma((experts,)),
            dma((experts,)),
            dma((experts,)),
            dma((experts,)),
            dma((replicas,)),
            dma((replicas,)),
            dma((chunks,)),
            dma((chunks,)),
            dma((chunks, chips)),
            dma((chunks, chips)),
            dma((chunks, chips)),
            dma((chunks, chips)),
            dma((chunks,)),
            dma((chunks,)),
            dma((experts,)),
            dma((experts,)),
        ],
        compiler_params=pltpu.CompilerParams(
            collective_id=0, has_side_effects=True, vmem_limit_bytes=60 * 1024 * 1024
        ),
    )(
        routes,
        route_weight,
        token_hidden.swapaxes(0, 1).reshape(tokens * top, width_ff),
        token_grad,
        gradient_eigenbasis[0],
        basis_hidden[0],
        query_grad[0],
        query_hidden[0],
        query_ids,
        jnp.broadcast_to(damping[:, None], (1, 128)),
    )
    scores = picked[:, :replicas].reshape(top, tokens, replicas).swapaxes(0, 1)
    return (scores, corrections[None])


def solution(mesh):
    torus = Mesh(
        mesh.devices.reshape(mesh.shape["expert"], 4, 2, 2), ("expert", "dp_0", "dp_1", "dp_2")
    )
    placed = (
        P(EXPERT_DP, None, None),
        P(EXPERT_DP, None),
        P(EXPERT_DP, None),
        P(EXPERT_DP, None),
        P("expert", None, None),
        P("expert", None, None),
        P("expert", DP, None),
        P("expert", DP, None),
        P("expert", DP),
        P("expert"),
    )
    return jax.shard_map(
        body,
        mesh=torus,
        in_specs=placed,
        out_specs=(P(EXPERT_DP, None, None), P("expert", DP, None)),
        check_vma=False,
    )
```

```python
import functools
import math

import jax
import jax.numpy as jnp
from jax import lax
from jax.experimental import pallas as pl
from jax.experimental.pallas import tpu as pltpu
from jax.sharding import Mesh
from jax.sharding import PartitionSpec as P

DP = ("dp_0", "dp_1", "dp_2")
EXPERT_DP = ("expert", "dp_0", "dp_1", "dp_2")

eps = 1e-06


MESH = pl.DeviceIdType.MESH
CHUNK = 128
ORDER = (
    ("C", 0), ("A", 2), ("C", 1), ("A", 3), ("E", 0), ("C", 2), ("A", 4), ("E", 1), ("C", 3),
    ("A", 5), ("R", 0), ("R", 1), ("S", 0, 0, 1), ("E", 2), ("C", 4), ("S", 0, 1, 3), ("E", 3),
    ("C", 5), ("S", 0, 3, 4), ("R", 2), ("R", 3), ("S", 1, 0, 2), ("E", 4), ("S", 1, 2, 4),
    ("E", 5), ("R", 4), ("R", 5), ("S", 2, 0, 4),
)


def back_kernel(
    scale,
    root,
    routes_ref,
    weight_ref,
    hidden_ref,
    grad_ref,
    basis_g_ref,
    basis_h_ref,
    query_g_ref,
    query_h_ref,
    ids_ref,
    damp_ref,
    out_ref,
    corr_ref,
    basis_g,
    basis_h,
    send_g,
    send_h,
    held_g,
    held_h,
    g_ref,
    h_ref,
    gsq,
    hsq,
    small,
    part,
    nearby,
    summed,
    far,
    inv,
    acc,
    ret_out,
    ret_in,
    basis_sem,
    dg_s,
    dg_r,
    dh_s,
    dh_r,
    small_s,
    small_r,
    core_s,
    core_r,
    rs_s,
    rs_r,
    ag_s,
    ag_r,
    cg_s,
    cg_r,
    ret_s,
    ret_r,
):
    e = lax.axis_index("expert")
    x = lax.axis_index("dp_0")
    z = lax.axis_index("dp_1")
    k = lax.axis_index("dp_2")
    xz = x * 2 + z
    chips = part.shape[2]
    experts = ret_out.shape[0]
    capacity = ret_out.shape[1]
    rows, width_d = g_ref.shape
    width_ff = h_ref.shape[1]
    chunks = width_ff // CHUNK
    bf16, f32 = jnp.bfloat16, jnp.float32

    def dp_id(index):
        return {"dp_0": index // 4, "dp_1": lax.rem(index // 2, 2), "dp_2": lax.rem(index, 2)}

    def chip_id(index):
        return {"dp_0": index // 2, "dp_1": lax.rem(index, 2)}

    me = xz * 2 + k
    barrier = pltpu.get_barrier_semaphore()

    def greet_dp(d, _):
        pl.semaphore_signal(
            barrier, 1, device_id=dp_id(lax.rem(me + d, 2 * chips)), device_id_type=MESH
        )
        return 0

    def greet_expert(d, _):
        pl.semaphore_signal(
            barrier, 1, device_id={"expert": lax.rem(e + d, experts)}, device_id_type=MESH
        )
        return 0

    lax.fori_loop(1, 2 * chips, greet_dp, 0)
    lax.fori_loop(1, experts, greet_expert, 0)
    load_g = pltpu.make_async_copy(basis_g_ref, basis_g, basis_sem.at[0])
    load_h = pltpu.make_async_copy(basis_h_ref, basis_h, basis_sem.at[1])
    load_g.start()
    load_h.start()

    def each(first, last, act):
        def once(d, _):
            act(d)
            return 0

        lax.fori_loop(first, last, once, 0)

    tokens = grad_ref.shape[0]
    top = routes_ref.shape[0]
    sent = tokens * top
    named = jnp.concatenate([routes_ref[j : j + 1, :] for j in range(top)], axis=1)
    onehot = (named == lax.broadcasted_iota(jnp.int32, (16, sent), 0)).astype(f32)

    def order_of(axis):
        index = lax.broadcasted_iota(jnp.int32, (sent, sent), axis)
        return jnp.where(index < tokens, index * top, (index - tokens) * top + 1)

    earlier = (order_of(0) < order_of(1)).astype(f32).astype(bf16)
    before = jnp.dot(onehot.astype(bf16), earlier, preferred_element_type=f32)
    within = jnp.sum(before * onehot, axis=0, keepdims=True).astype(jnp.int32)
    slots = named * capacity + within
    chosen = (slots == lax.broadcasted_iota(jnp.int32, (experts * capacity, sent), 0)).astype(f32)
    weights = jnp.concatenate([weight_ref[j : j + 1, :] for j in range(top)], axis=1)
    weight = jnp.sum(chosen * weights, axis=1, keepdims=True)
    picks = [chosen[:, j * tokens : (j + 1) * tokens].astype(bf16) for j in range(top)]
    gathered = jnp.dot(sum(picks[1:], picks[0]), grad_ref[...], preferred_element_type=f32)
    send_g[...] = (weight * gathered).astype(bf16).reshape(send_g.shape)

    def dispatch_copy(source, target, ssem, rsem, d):
        to = lax.rem(e + d, experts)
        return pltpu.make_async_remote_copy(
            source.at[to],
            target.at[d],
            ssem.at[d],
            rsem.at[d],
            device_id={"expert": to},
            device_id_type=MESH,
        )

    def dg_copy(d):
        return dispatch_copy(send_g, held_g, dg_s, dg_r, d)

    def dh_copy(d):
        return dispatch_copy(send_h, held_h, dh_s, dh_r, d)

    pl.semaphore_wait(barrier, 2 * chips - 1 + experts - 1)
    each(1, experts, lambda d: dg_copy(d).start())
    hidden = hidden_ref[...].astype(f32)
    moved = None
    for j in range(top):
        part_j = jnp.dot(picks[j], hidden[:, j, :].astype(bf16), preferred_element_type=f32)
        moved = part_j if moved is None else moved + part_j
    send_h[...] = moved.astype(bf16).reshape(send_h.shape)
    each(1, experts, lambda d: dh_copy(d).start())
    acc[...] = jnp.zeros_like(acc)

    def rotate(value, basis, rotated, squared, first):
        turned = jnp.dot(value, basis[...], preferred_element_type=f32).astype(bf16)
        count = value.shape[0]
        rotated[first : first + count, :] = turned
        square = jnp.square(turned.astype(f32)).astype(bf16)
        squared[first : first + count, :] = square
        return jnp.sum(square.astype(f32), axis=1, keepdims=True)

    load_h.wait()
    load_g.wait()
    row_g = [rotate(send_g[e], basis_g, g_ref, gsq, 0)]
    query_row = lax.broadcasted_iota(jnp.int32, (query_g_ref.shape[0], 1), 0) == ids_ref[0, 0]

    def query(ref, basis):
        turned = jnp.dot(ref[...], basis[...], preferred_element_type=f32)
        one = jnp.sum(jnp.where(query_row, turned, 0.0), axis=0, keepdims=True)
        return one.astype(bf16).astype(f32)

    query_g = query(query_g_ref, basis_g)
    query_h = query(query_h_ref, basis_h)
    for first, last in ((1, experts // 2), (experts // 2, experts)):
        each(first, last, lambda d: dg_copy(d).wait_recv())
        row_g.append(
            rotate(
                held_g[first:last].reshape((last - first) * capacity, width_d),
                basis_g,
                g_ref,
                gsq,
                first * capacity,
            )
        )
    each(1, experts, lambda d: dh_copy(d).wait_recv())
    row_h = rotate(
        jnp.concatenate(
            [send_h[e], held_h[1:experts].reshape((experts - 1) * capacity, width_ff)], axis=0
        ),
        basis_h,
        h_ref,
        hsq,
        0,
    )

    def core_copy(c):
        return pltpu.make_async_remote_copy(
            part.at[c, 1 - k],
            nearby.at[c],
            core_s.at[c],
            core_r.at[c],
            device_id={"dp_2": 1 - k},
            device_id_type=MESH,
        )

    def rs_copy(c, d):
        to = lax.rem(xz + d, chips)
        return pltpu.make_async_remote_copy(
            summed.at[c, to],
            far.at[c, d],
            rs_s.at[c, d],
            rs_r.at[c, d],
            device_id=chip_id(to),
            device_id_type=MESH,
        )

    def ag_copy(c, d):
        to = lax.rem(xz + d, chips)
        return pltpu.make_async_remote_copy(
            inv.at[c, k, xz],
            inv.at[c, k, xz],
            ag_s.at[c, d],
            ag_r.at[c, d],
            device_id=chip_id(to),
            device_id_type=MESH,
        )

    def ag_arrival(c, d):
        origin = lax.rem(xz + chips - d, chips)
        return pltpu.make_async_remote_copy(
            inv.at[c, k, origin],
            inv.at[c, k, origin],
            ag_s.at[c, d],
            ag_r.at[c, d],
            device_id=chip_id(origin),
            device_id_type=MESH,
        )

    def cg_copy(c, side):
        return pltpu.make_async_remote_copy(
            inv.at[c, side],
            inv.at[c, side],
            cg_s.at[c],
            cg_r.at[c],
            device_id={"dp_2": 1 - k},
            device_id_type=MESH,
        )

    def small_copy(d, slot):
        return pltpu.make_async_remote_copy(
            small.at[me],
            small.at[slot],
            small_s.at[d],
            small_r.at[d],
            device_id=dp_id(lax.rem(me + d, 2 * chips)),
            device_id_type=MESH,
        )

    def spread(pair):
        both = lax.dot_general(
            hsq[:, pair * 2 * CHUNK : (pair + 1) * 2 * CHUNK],
            gsq[...],
            (((0,), (0,)), ((), ())),
            preferred_element_type=f32,
        ).astype(bf16)
        for half in range(2):
            for q in range(2 * chips):
                part[2 * pair + half, q % 2, q // 2] = both[
                    half * CHUNK : (half + 1) * CHUNK, q * CHUNK : (q + 1) * CHUNK
                ]
            core_copy(2 * pair + half).start()

    def share():
        own_sum = jnp.sum(jnp.concatenate(row_g, axis=0) * row_h, axis=0, keepdims=True)
        for j in range(width_d // 128):
            small[me, j : j + 1, :] = query_g[:, j * 128 : (j + 1) * 128]
        for j in range(width_ff // 128):
            small[me, 16 + j : 17 + j, :] = query_h[:, j * 128 : (j + 1) * 128]
        small[me, 22:24, :] = jnp.broadcast_to(own_sum, (2, 128))
        each(1, 2 * chips, lambda d: small_copy(d, me).start())

    def stage_one(c):
        core_copy(c).wait()
        summed[c] = (part[c, k].astype(f32) + nearby[c].astype(f32)).astype(bf16)
        each(1, chips, lambda d: rs_copy(c, d).start())

    def stage_two(c, level):
        each(1, chips, lambda d: rs_copy(c, d).wait_recv())
        total = summed[c, xz].astype(f32)
        for d in range(1, chips):
            total = total + far[c, d].astype(f32)
        block = total.T * scale
        corr_ref[:, c * CHUNK : (c + 1) * CHUNK] = block
        inv[c, k, xz] = (1.0 / (block + level)).astype(bf16)
        each(1, chips, lambda d: ag_copy(c, d).start())

    def stage_three(c):
        each(1, chips, lambda d: ag_arrival(c, d).wait_recv())
        cg_copy(c, k).start()

    def ready(c):
        cg_copy(c, 1 - k).wait_recv()

    lane = lax.broadcasted_iota(jnp.int32, acc.shape, 1)
    group = 4

    def score(pair, first, last):
        def step(t, _):
            parts = []
            for j in range(group):
                n = t * group + j
                pieces = []
                for q in range(2 * chips):
                    d = (q % chips) * 2 + q // chips
                    pieces.append(
                        g_ref[:, d * CHUNK : (d + 1) * CHUNK]
                        * small[n, d : d + 1, :].astype(bf16)
                    )
                parts.append(jnp.concatenate(pieces, axis=1))
            scaled = jnp.concatenate(parts, axis=0)
            weights = jnp.concatenate(
                [inv[2 * pair + half].reshape(width_d, CHUNK) for half in range(2)], axis=1
            )
            product = jnp.dot(scaled, weights, preferred_element_type=f32)
            total = acc[...]
            for j in range(group):
                n = t * group + j
                value = None
                for half in range(2):
                    c = 2 * pair + half
                    term = product[
                        j * rows : (j + 1) * rows, half * CHUNK : (half + 1) * CHUNK
                    ] * (
                        h_ref[:, c * CHUNK : (c + 1) * CHUNK].astype(f32)
                        * small[n, 16 + c : 17 + c, :]
                    )
                    value = term if value is None else value + term
                total = total + jnp.where(
                    lane == n, jnp.sum(value, axis=1, keepdims=True), 0.0
                )
            acc[...] = total
            return 0

        lax.fori_loop(first, last, step, 0)

    def small_arrival(d):
        small_copy(d, lax.rem(me + 2 * chips - d, 2 * chips)).wait_recv()

    spread(0)
    share()
    spread(1)
    stage_one(0)
    stage_one(1)
    spread(2)
    each(1, 2 * chips, small_arrival)
    complete = small[0, 22:23, :]
    for n in range(1, 2 * chips):
        complete = complete + small[n, 22:23, :]
    level = damp_ref[0] * (complete * (scale / (width_d * width_ff)) + eps)

    stages = {"A": stage_one, "C": lambda c: stage_two(c, level), "E": stage_three, "R": ready}
    for act, c, *span in ORDER:
        if act == "S":
            score(c, *span)
        else:
            stages[act](c)

    ret_out[...] = (acc[...] / root).reshape(ret_out.shape)

    def ret_copy(d, slot):
        return pltpu.make_async_remote_copy(
            ret_out.at[d],
            ret_in.at[slot],
            ret_s.at[d],
            ret_r.at[d],
            device_id={"expert": lax.rem(e + experts - d, experts)},
            device_id_type=MESH,
        )

    each(1, experts, lambda d: ret_copy(d, e).start())
    ret_in[e] = ret_out[0]
    each(1, experts, lambda d: ret_copy(d, lax.rem(e + d, experts)).wait_recv())
    result = lax.dot_general(
        ret_in[...].reshape(experts * capacity, -1),
        chosen,
        (((0,), (0,)), ((), ())),
        preferred_element_type=f32,
        precision=lax.Precision.HIGHEST,
    )
    for j in range(top):
        out_ref[j] = result[: out_ref.shape[1], j * tokens : (j + 1) * tokens]
    for c in range(chunks):
        each(1, chips, lambda d: rs_copy(c, d).wait_send())
        each(1, chips, lambda d: ag_copy(c, d).wait_send())
        cg_copy(c, k).wait_send()
    each(1, 2 * chips, lambda d: small_copy(d, me).wait_send())
    each(1, experts, lambda d: ret_copy(d, e).wait_send())
    each(1, experts, lambda d: dg_copy(d).wait_send())
    each(1, experts, lambda d: dh_copy(d).wait_send())


def body(
    token_hidden,
    token_grad,
    routes,
    route_weight,
    gradient_eigenbasis,
    basis_hidden,
    query_hidden,
    query_grad,
    query_ids,
    damping,
):
    experts = lax.axis_size("expert")
    replicas = lax.axis_size(DP)
    tokens, top, width_ff = token_hidden.shape
    width_d = token_grad.shape[1]
    capacity = tokens * top * 3 // (2 * experts)
    rows = experts * capacity
    chips = replicas // 2
    chunks = width_ff // CHUNK
    bf16, f32 = jnp.bfloat16, jnp.float32
    block = width_d // replicas
    dma = pltpu.SemaphoreType.DMA
    vmem = pl.BlockSpec(memory_space=pltpu.VMEM)
    anywhere = pl.BlockSpec(memory_space=pl.ANY)
    smem = pl.BlockSpec(memory_space=pltpu.SMEM)
    picked, corrections = pl.pallas_call(
        functools.partial(
            back_kernel, 1.0 / (replicas * experts * capacity), math.sqrt(width_d * width_ff)
        ),
        out_shape=(
            jax.ShapeDtypeStruct((top, replicas, tokens), f32),
            jax.ShapeDtypeStruct((block, width_ff), f32),
        ),
        in_specs=[vmem] * 4 + [anywhere] * 2 + [vmem] * 2 + [smem] * 2,
        out_specs=(vmem, vmem),
        scratch_shapes=[
            pltpu.VMEM((width_d, width_d), bf16),
            pltpu.VMEM((width_ff, width_ff), bf16),
            pltpu.VMEM((experts, capacity, width_d), bf16),
            pltpu.VMEM((experts, capacity, width_ff), bf16),
            pltpu.VMEM((experts, capacity, width_d), bf16),
            pltpu.VMEM((experts, capacity, width_ff), bf16),
            pltpu.VMEM((rows, width_d), bf16),
            pltpu.VMEM((rows, width_ff), bf16),
            pltpu.VMEM((rows, width_d), bf16),
            pltpu.VMEM((rows, width_ff), bf16),
            pltpu.VMEM((replicas, 24, 128), f32),
            pltpu.VMEM((chunks, 2, chips, CHUNK, block), bf16),
            pltpu.VMEM((chunks, chips, CHUNK, block), bf16),
            pltpu.VMEM((chunks, chips, CHUNK, block), bf16),
            pltpu.VMEM((chunks, chips, CHUNK, block), bf16),
            pltpu.VMEM((chunks, 2, chips, block, CHUNK), bf16),
            pltpu.VMEM((rows, 128), f32),
            pltpu.VMEM((experts, capacity, 128), f32),
            pltpu.VMEM((experts, capacity, 128), f32),
            dma((2,)),
            dma((experts,)),
            dma((experts,)),
            dma((experts,)),
            dma((experts,)),
            dma((replicas,)),
            dma((replicas,)),
            dma((chunks,)),
            dma((chunks,)),
            dma((chunks, chips)),
            dma((chunks, chips)),
            dma((chunks, chips)),
            dma((chunks, chips)),
            dma((chunks,)),
            dma((chunks,)),
            dma((experts,)),
            dma((experts,)),
        ],
        compiler_params=pltpu.CompilerParams(
            collective_id=0, has_side_effects=True, vmem_limit_bytes=60 * 1024 * 1024
        ),
    )(
        routes.T,
        route_weight.T,
        token_hidden,
        token_grad,
        gradient_eigenbasis[0],
        basis_hidden[0],
        query_grad[0],
        query_hidden[0],
        query_ids,
        damping,
    )
    return (picked.transpose(2, 0, 1), corrections[None])


def solution(mesh):
    torus = Mesh(
        mesh.devices.reshape(mesh.shape["expert"], 4, 2, 2), ("expert", "dp_0", "dp_1", "dp_2")
    )
    placed = (
        P(EXPERT_DP, None, None),
        P(EXPERT_DP, None),
        P(EXPERT_DP, None),
        P(EXPERT_DP, None),
        P("expert", None, None),
        P("expert", None, None),
        P("expert", DP, None),
        P("expert", DP, None),
        P("expert", DP),
        P("expert"),
    )
    return jax.shard_map(
        body,
        mesh=torus,
        in_specs=placed,
        out_specs=(P(EXPERT_DP, None, None), P("expert", DP, None)),
        check_vma=False,
    )
```

```python
import functools
import math

import jax
import jax.numpy as jnp
from jax import lax
from jax.experimental import pallas as pl
from jax.experimental.pallas import tpu as pltpu
from jax.sharding import Mesh
from jax.sharding import PartitionSpec as P

DP = ("dp_0", "dp_1", "dp_2")
EXPERT_DP = ("expert", "dp_0", "dp_1", "dp_2")

eps = 1e-06


MESH = pl.DeviceIdType.MESH
CHUNK = 128
ORDER = (
    ("C", 0), ("A", 2), ("C", 1), ("A", 3), ("E", 0), ("C", 2), ("A", 4), ("E", 1), ("R", 0),
    ("R", 1), ("S", 0, 0, 1), ("C", 3), ("A", 5), ("S", 0, 1, 2), ("E", 2), ("S", 0, 2, 4),
    ("C", 4), ("E", 3), ("R", 2), ("R", 3), ("S", 1, 0, 1), ("C", 5), ("S", 1, 1, 3), ("E", 4),
    ("S", 1, 3, 4), ("E", 5), ("R", 4), ("R", 5), ("S", 2, 0, 4),
)


def back_kernel(
    scale,
    root,
    routes_ref,
    weight_ref,
    hidden_ref,
    grad_ref,
    basis_g_ref,
    basis_h_ref,
    query_g_ref,
    query_h_ref,
    ids_ref,
    damp_ref,
    out_ref,
    corr_ref,
    basis_g,
    basis_h,
    token_hidden,
    token_grad,
    query_rows_g,
    query_rows_h,
    send_g,
    send_h,
    held_g,
    held_h,
    g_ref,
    h_ref,
    gsq,
    hsq,
    small,
    sums,
    back,
    part,
    nearby,
    summed,
    far,
    inv,
    acc,
    ret_out,
    ret_in,
    basis_sem,
    dg_s,
    dg_r,
    dh_s,
    dh_r,
    small_s,
    small_r,
    ask_s,
    ask_r,
    core_s,
    core_r,
    rs_s,
    rs_r,
    ag_s,
    ag_r,
    cg_s,
    cg_r,
    ret_s,
    ret_r,
):
    e = lax.axis_index("expert")
    x = lax.axis_index("dp_0")
    z = lax.axis_index("dp_1")
    k = lax.axis_index("dp_2")
    xz = x * 2 + z
    chips = part.shape[2]
    experts = ret_out.shape[0]
    capacity = held_g.shape[1]
    rows, width_d = g_ref.shape
    width_ff = h_ref.shape[1]
    chunks = width_ff // CHUNK
    bf16, f32 = jnp.bfloat16, jnp.float32

    def dp_id(index):
        return {"dp_0": index // 4, "dp_1": lax.rem(index // 2, 2), "dp_2": lax.rem(index, 2)}

    def chip_id(index):
        return {"dp_0": index // 2, "dp_1": lax.rem(index, 2)}

    me = xz * 2 + k
    barrier = pltpu.get_barrier_semaphore()

    def greet_dp(d, _):
        pl.semaphore_signal(
            barrier, 1, device_id=dp_id(lax.rem(me + d, 2 * chips)), device_id_type=MESH
        )
        return 0

    def greet_expert(d, _):
        pl.semaphore_signal(
            barrier, 1, device_id={"expert": lax.rem(e + d, experts)}, device_id_type=MESH
        )
        return 0

    lax.fori_loop(1, 2 * chips, greet_dp, 0)
    lax.fori_loop(1, experts, greet_expert, 0)
    loads = [
        pltpu.make_async_copy(source, target, basis_sem.at[index])
        for index, (source, target) in enumerate(
            (
                (grad_ref, token_grad),
                (hidden_ref, token_hidden),
                (query_g_ref, query_rows_g),
                (query_h_ref, query_rows_h),
                (basis_h_ref, basis_h),
                (basis_g_ref, basis_g),
            )
        )
    ]
    for load in loads:
        load.start()

    def each(first, last, act):
        def once(d, _):
            act(d)
            return 0

        lax.fori_loop(first, last, once, 0)

    tokens = grad_ref.shape[0]
    top = routes_ref.shape[0]
    sent = tokens * top
    named = jnp.concatenate([routes_ref[j : j + 1, :] for j in range(top)], axis=1)
    onehot = (named == lax.broadcasted_iota(jnp.int32, (16, sent), 0)).astype(f32)

    def order_of(axis):
        index = lax.broadcasted_iota(jnp.int32, (sent, sent), axis)
        return jnp.where(index < tokens, index * top, (index - tokens) * top + 1)

    earlier = (order_of(0) < order_of(1)).astype(f32).astype(bf16)
    before = jnp.dot(onehot.astype(bf16), earlier, preferred_element_type=f32)
    within = jnp.sum(before * onehot, axis=0, keepdims=True).astype(jnp.int32)
    slots = named * capacity + within
    chosen = (slots == lax.broadcasted_iota(jnp.int32, (experts * capacity, sent), 0)).astype(f32)
    weights = jnp.concatenate([weight_ref[j : j + 1, :] for j in range(top)], axis=1)
    weight = jnp.sum(chosen * weights, axis=1, keepdims=True)
    picks = [chosen[:, j * tokens : (j + 1) * tokens].astype(bf16) for j in range(top)]
    loads[0].wait()
    gathered = jnp.dot(sum(picks[1:], picks[0]), token_grad[...], preferred_element_type=f32)
    send_g[...] = (weight * gathered).astype(bf16).reshape(send_g.shape)

    def dispatch_copy(source, target, ssem, rsem, d):
        to = lax.rem(e + d, experts)
        return pltpu.make_async_remote_copy(
            source.at[to],
            target.at[d],
            ssem.at[d],
            rsem.at[d],
            device_id={"expert": to},
            device_id_type=MESH,
        )

    def dg_copy(d):
        return dispatch_copy(send_g, held_g, dg_s, dg_r, d)

    def dh_copy(d):
        return dispatch_copy(send_h, held_h, dh_s, dh_r, d)

    pl.semaphore_wait(barrier, 2 * chips - 1 + experts - 1)
    each(1, experts, lambda d: dg_copy(d).start())
    loads[1].wait()
    hidden = token_hidden[...].astype(f32)
    moved = None
    for j in range(top):
        part_j = jnp.dot(picks[j], hidden[:, j, :].astype(bf16), preferred_element_type=f32)
        moved = part_j if moved is None else moved + part_j
    send_h[...] = moved.astype(bf16).reshape(send_h.shape)
    each(1, experts, lambda d: dh_copy(d).start())
    acc[...] = jnp.zeros_like(acc)
    back[...] = jnp.zeros_like(back)
    for j in range(experts):
        back[j, :capacity, :] = chosen[j * capacity : (j + 1) * capacity].astype(bf16)

    def rotate(value, basis, rotated, squared, first):
        turned = jnp.dot(value, basis[...], preferred_element_type=f32).astype(bf16)
        count = value.shape[0]
        rotated[first : first + count, :] = turned
        square = jnp.square(turned.astype(f32)).astype(bf16)
        squared[first : first + count, :] = square
        return jnp.sum(square.astype(f32), axis=1, keepdims=True)

    for load in loads[2:]:
        load.wait()
    row_g = [rotate(send_g[e], basis_g, g_ref, gsq, 0)]
    query_row = lax.broadcasted_iota(jnp.int32, (query_g_ref.shape[0], 1), 0) == ids_ref[0, 0]

    def query(ref, basis):
        turned = jnp.dot(ref[...], basis[...], preferred_element_type=f32)
        one = jnp.sum(jnp.where(query_row, turned, 0.0), axis=0, keepdims=True)
        return one.astype(bf16).astype(f32)

    query_g = query(query_rows_g, basis_g)
    query_h = query(query_rows_h, basis_h)
    for j in range(width_d // 128):
        small[k, x, z, j : j + 1, :] = query_g[:, j * 128 : (j + 1) * 128]
    for j in range(width_ff // 128):
        small[k, x, z, 16 + j : 17 + j, :] = query_h[:, j * 128 : (j + 1) * 128]

    def ask_near(half):
        return pltpu.make_async_remote_copy(
            small.at[k, x, half],
            small.at[k, x, half],
            ask_s.at[0],
            ask_r.at[0],
            device_id={"dp_1": 1 - z},
            device_id_type=MESH,
        )

    def ask_line(d, line):
        return pltpu.make_async_remote_copy(
            small.at[k, line],
            small.at[k, line],
            ask_s.at[d],
            ask_r.at[d],
            device_id={"dp_0": lax.rem(x + d, 4)},
            device_id_type=MESH,
        )

    def ask_core(side):
        return pltpu.make_async_remote_copy(
            small.at[side],
            small.at[side],
            ask_s.at[4],
            ask_r.at[4],
            device_id={"dp_2": 1 - k},
            device_id_type=MESH,
        )

    ask_near(z).start()
    for first, last in ((1, experts // 2), (experts // 2, experts)):
        each(first, last, lambda d: dg_copy(d).wait_recv())
        row_g.append(
            rotate(
                held_g[first:last].reshape((last - first) * capacity, width_d),
                basis_g,
                g_ref,
                gsq,
                first * capacity,
            )
        )
        if first == 1:
            ask_near(1 - z).wait_recv()
            each(1, 4, lambda d: ask_line(d, x).start())
        else:
            each(1, 4, lambda d: ask_line(d, lax.rem(x + 4 - d, 4)).wait_recv())
            ask_core(k).start()
    each(1, experts, lambda d: dh_copy(d).wait_recv())
    row_h = rotate(
        jnp.concatenate(
            [send_h[e], held_h[1:experts].reshape((experts - 1) * capacity, width_ff)], axis=0
        ),
        basis_h,
        h_ref,
        hsq,
        0,
    )

    def core_copy(c):
        return pltpu.make_async_remote_copy(
            part.at[c, 1 - k],
            nearby.at[c],
            core_s.at[c],
            core_r.at[c],
            device_id={"dp_2": 1 - k},
            device_id_type=MESH,
        )

    def rs_copy(c, d):
        to = lax.rem(xz + d, chips)
        return pltpu.make_async_remote_copy(
            summed.at[c, to],
            far.at[c, d],
            rs_s.at[c, d],
            rs_r.at[c, d],
            device_id=chip_id(to),
            device_id_type=MESH,
        )

    def ag_copy(c, d):
        to = lax.rem(xz + d, chips)
        return pltpu.make_async_remote_copy(
            inv.at[c, k, xz],
            inv.at[c, k, xz],
            ag_s.at[c, d],
            ag_r.at[c, d],
            device_id=chip_id(to),
            device_id_type=MESH,
        )

    def ag_arrival(c, d):
        origin = lax.rem(xz + chips - d, chips)
        return pltpu.make_async_remote_copy(
            inv.at[c, k, origin],
            inv.at[c, k, origin],
            ag_s.at[c, d],
            ag_r.at[c, d],
            device_id=chip_id(origin),
            device_id_type=MESH,
        )

    def cg_copy(c, side):
        return pltpu.make_async_remote_copy(
            inv.at[c, side],
            inv.at[c, side],
            cg_s.at[c],
            cg_r.at[c],
            device_id={"dp_2": 1 - k},
            device_id_type=MESH,
        )

    def small_copy(d, slot):
        return pltpu.make_async_remote_copy(
            sums.at[me],
            sums.at[slot],
            small_s.at[d],
            small_r.at[d],
            device_id=dp_id(lax.rem(me + d, 2 * chips)),
            device_id_type=MESH,
        )

    def spread(pair):
        both = lax.dot_general(
            hsq[:, pair * 2 * CHUNK : (pair + 1) * 2 * CHUNK],
            gsq[...],
            (((0,), (0,)), ((), ())),
            preferred_element_type=f32,
        ).astype(bf16)
        for half in range(2):
            for q in range(2 * chips):
                part[2 * pair + half, q % 2, q // 2] = both[
                    half * CHUNK : (half + 1) * CHUNK, q * CHUNK : (q + 1) * CHUNK
                ]
            core_copy(2 * pair + half).start()

    def share():
        own_sum = jnp.sum(jnp.concatenate(row_g, axis=0) * row_h, axis=0, keepdims=True)
        sums[me] = jnp.broadcast_to(own_sum, (8, 128))
        each(1, 2 * chips, lambda d: small_copy(d, me).start())

    def stage_one(c):
        core_copy(c).wait()
        summed[c] = (part[c, k].astype(f32) + nearby[c].astype(f32)).astype(bf16)
        each(1, chips, lambda d: rs_copy(c, d).start())

    def stage_two(c, level):
        each(1, chips, lambda d: rs_copy(c, d).wait_recv())
        total = summed[c, xz].astype(f32)
        for d in range(1, chips):
            total = total + far[c, d].astype(f32)
        block = total.T * scale
        corr_ref[:, c * CHUNK : (c + 1) * CHUNK] = block
        inv[c, k, xz] = (1.0 / (block + level)).astype(bf16)
        each(1, chips, lambda d: ag_copy(c, d).start())

    def stage_three(c):
        each(1, chips, lambda d: ag_arrival(c, d).wait_recv())
        cg_copy(c, k).start()

    def ready(c):
        cg_copy(c, 1 - k).wait_recv()

    lane = lax.broadcasted_iota(jnp.int32, acc.shape, 1)
    group = 4

    def score(pair, first, last):
        def step(t, _):
            parts = []
            for j in range(group):
                pieces = []
                for q in range(2 * chips):
                    d = (q % chips) * 2 + q // chips
                    pieces.append(
                        g_ref[:, d * CHUNK : (d + 1) * CHUNK]
                        * small[j % 2, t, j // 2, d : d + 1, :].astype(bf16)
                    )
                parts.append(jnp.concatenate(pieces, axis=1))
            scaled = jnp.concatenate(parts, axis=0)
            weights = jnp.concatenate(
                [inv[2 * pair + half].reshape(width_d, CHUNK) for half in range(2)], axis=1
            )
            product = jnp.dot(scaled, weights, preferred_element_type=f32)
            total = acc[...]
            for j in range(group):
                n = t * group + j
                value = None
                for half in range(2):
                    c = 2 * pair + half
                    term = product[
                        j * rows : (j + 1) * rows, half * CHUNK : (half + 1) * CHUNK
                    ] * (
                        h_ref[:, c * CHUNK : (c + 1) * CHUNK].astype(f32)
                        * small[j % 2, t, j // 2, 16 + c : 17 + c, :]
                    )
                    value = term if value is None else value + term
                total = total + jnp.where(
                    lane == n, jnp.sum(value, axis=1, keepdims=True), 0.0
                )
            acc[...] = total
            return 0

        lax.fori_loop(first, last, step, 0)

    def small_arrival(d):
        small_copy(d, lax.rem(me + 2 * chips - d, 2 * chips)).wait_recv()

    spread(0)
    share()
    spread(1)
    stage_one(0)
    stage_one(1)
    spread(2)
    each(1, 2 * chips, small_arrival)
    complete = sums[0, 0:1, :]
    for n in range(1, 2 * chips):
        complete = complete + sums[n, 0:1, :]
    level = damp_ref[0] * (complete * (scale / (width_d * width_ff)) + eps)

    ask_core(1 - k).wait_recv()
    stages = {"A": stage_one, "C": lambda c: stage_two(c, level), "E": stage_three, "R": ready}
    for act, c, *span in ORDER:
        if act == "S":
            score(c, *span)
        else:
            stages[act](c)

    turned_scores = (acc[...] / root).T[: ret_out.shape[1], :]
    blank = jnp.zeros((ret_out.shape[1], 128 - capacity), f32)
    for d in range(experts):
        ret_out[d] = jnp.concatenate(
            [turned_scores[:, d * capacity : (d + 1) * capacity], blank], axis=1
        )

    def ret_copy(d, slot):
        return pltpu.make_async_remote_copy(
            ret_out.at[d],
            ret_in.at[slot],
            ret_s.at[d],
            ret_r.at[d],
            device_id={"expert": lax.rem(e + experts - d, experts)},
            device_id_type=MESH,
        )

    each(1, experts, lambda d: ret_copy(d, e).start())
    ret_in[e] = ret_out[0]
    for c in range(chunks):
        each(1, chips, lambda d: rs_copy(c, d).wait_send())
        each(1, chips, lambda d: ag_copy(c, d).wait_send())
        cg_copy(c, k).wait_send()
    each(1, 2 * chips, lambda d: small_copy(d, me).wait_send())
    ask_near(z).wait_send()
    each(1, 4, lambda d: ask_line(d, x).wait_send())
    ask_core(k).wait_send()
    each(1, experts, lambda d: dg_copy(d).wait_send())
    each(1, experts, lambda d: dh_copy(d).wait_send())
    each(1, experts, lambda d: ret_copy(d, lax.rem(e + d, experts)).wait_recv())
    arrived = jnp.concatenate([ret_in[j] for j in range(experts)], axis=1)
    high = arrived.astype(bf16)
    rest = arrived - high.astype(f32)
    middle = rest.astype(bf16)
    low = (rest - middle.astype(f32)).astype(bf16)
    result = jnp.dot(
        jnp.concatenate([high, middle, low], axis=0),
        back[...].reshape(experts * 128, sent),
        preferred_element_type=f32,
    )
    queries = ret_out.shape[1]
    result = result[:queries] + result[queries : 2 * queries] + result[2 * queries :]
    for j in range(top):
        out_ref[j] = result[:, j * tokens : (j + 1) * tokens]
    each(1, experts, lambda d: ret_copy(d, e).wait_send())


def write_kernel(picked_ref, sums_ref, scores_ref, corr_ref):
    scores_ref[...] = picked_ref[...]
    corr_ref[...] = sums_ref[...]


def body(
    token_hidden,
    token_grad,
    routes,
    route_weight,
    gradient_eigenbasis,
    basis_hidden,
    query_hidden,
    query_grad,
    query_ids,
    damping,
):
    experts = lax.axis_size("expert")
    replicas = lax.axis_size(DP)
    tokens, top, width_ff = token_hidden.shape
    width_d = token_grad.shape[1]
    capacity = tokens * top * 3 // (2 * experts)
    rows = experts * capacity
    chips = replicas // 2
    chunks = width_ff // CHUNK
    bf16, f32 = jnp.bfloat16, jnp.float32
    block = width_d // replicas
    dma = pltpu.SemaphoreType.DMA
    vmem = pl.BlockSpec(memory_space=pltpu.VMEM)
    anywhere = pl.BlockSpec(memory_space=pl.ANY)
    smem = pl.BlockSpec(memory_space=pltpu.SMEM)
    picked, corrections = pl.pallas_call(
        functools.partial(
            back_kernel, 1.0 / (replicas * experts * capacity), math.sqrt(width_d * width_ff)
        ),
        out_shape=(
            jax.ShapeDtypeStruct((top, replicas, tokens), f32),
            jax.ShapeDtypeStruct((block, width_ff), f32),
        ),
        in_specs=[vmem] * 2 + [anywhere] * 6 + [smem] * 2,
        out_specs=(vmem, vmem),
        scratch_shapes=[
            pltpu.VMEM((width_d, width_d), bf16),
            pltpu.VMEM((width_ff, width_ff), bf16),
            pltpu.VMEM(token_hidden.shape, bf16),
            pltpu.VMEM(token_grad.shape, bf16),
            pltpu.VMEM(query_grad.shape[1:], bf16),
            pltpu.VMEM(query_hidden.shape[1:], bf16),
            pltpu.VMEM((experts, capacity, width_d), bf16),
            pltpu.VMEM((experts, capacity, width_ff), bf16),
            pltpu.VMEM((experts, capacity, width_d), bf16),
            pltpu.VMEM((experts, capacity, width_ff), bf16),
            pltpu.VMEM((rows, width_d), bf16),
            pltpu.VMEM((rows, width_ff), bf16),
            pltpu.VMEM((rows, width_d), bf16),
            pltpu.VMEM((rows, width_ff), bf16),
            pltpu.VMEM((2, chips // 2, 2, 24, 128), f32),
            pltpu.VMEM((replicas, 8, 128), f32),
            pltpu.VMEM((experts, 128, tokens * top), bf16),
            pltpu.VMEM((chunks, 2, chips, CHUNK, block), bf16),
            pltpu.VMEM((chunks, chips, CHUNK, block), bf16),
            pltpu.VMEM((chunks, chips, CHUNK, block), bf16),
            pltpu.VMEM((chunks, chips, CHUNK, block), bf16),
            pltpu.VMEM((chunks, 2, chips, block, CHUNK), bf16),
            pltpu.VMEM((rows, 128), f32),
            pltpu.VMEM((experts, replicas, 128), f32),
            pltpu.VMEM((experts, replicas, 128), f32),
            dma((6,)),
            dma((experts,)),
            dma((experts,)),
            dma((experts,)),
            dma((experts,)),
            dma((replicas,)),
            dma((replicas,)),
            dma((5,)),
            dma((5,)),
            dma((chunks,)),
            dma((chunks,)),
            dma((chunks, chips)),
            dma((chunks, chips)),
            dma((chunks, chips)),
            dma((chunks, chips)),
            dma((chunks,)),
            dma((chunks,)),
            dma((experts,)),
            dma((experts,)),
        ],
        compiler_params=pltpu.CompilerParams(
            collective_id=0, has_side_effects=True, vmem_limit_bytes=60 * 1024 * 1024
        ),
    )(
        routes.T,
        route_weight.T,
        token_hidden,
        token_grad,
        gradient_eigenbasis[0],
        basis_hidden[0],
        query_grad[0],
        query_hidden[0],
        query_ids,
        damping,
    )
    picked, corrections = pl.pallas_call(
        write_kernel,
        out_shape=tuple(jax.ShapeDtypeStruct(a.shape, f32) for a in (picked, corrections)),
        in_specs=[vmem] * 2,
        out_specs=(vmem, vmem),
        compiler_params=pltpu.CompilerParams(vmem_limit_bytes=2 * 1024 * 1024),
    )(picked, corrections)
    return (picked.transpose(2, 0, 1), corrections[None])


def solution(mesh):
    torus = Mesh(
        mesh.devices.reshape(mesh.shape["expert"], 4, 2, 2), ("expert", "dp_0", "dp_1", "dp_2")
    )
    placed = (
        P(EXPERT_DP, None, None),
        P(EXPERT_DP, None),
        P(EXPERT_DP, None),
        P(EXPERT_DP, None),
        P("expert", None, None),
        P("expert", None, None),
        P("expert", DP, None),
        P("expert", DP, None),
        P("expert", DP),
        P("expert"),
    )
    return jax.shard_map(
        body,
        mesh=torus,
        in_specs=placed,
        out_specs=(P(EXPERT_DP, None, None), P("expert", DP, None)),
        check_vma=False,
    )
```

```python
import functools
import math

import jax
import jax.numpy as jnp
from jax import lax
from jax.experimental import pallas as pl
from jax.experimental.pallas import tpu as pltpu
from jax.sharding import Mesh
from jax.sharding import PartitionSpec as P

DP = ("dp_0", "dp_1", "dp_2")
EXPERT_DP = ("expert", "dp_0", "dp_1", "dp_2")

eps = 1e-06


MESH = pl.DeviceIdType.MESH
CHUNK = 128
ORDER = (
    ("C", 0), ("C", 1), ("A", 2), ("A", 3), ("E", 0), ("E", 1), ("R", 0), ("R", 1), ("S", 0, 0, 1),
    ("C", 2), ("S", 0, 1, 2), ("C", 3), ("A", 4), ("S", 0, 2, 4), ("E", 2), ("A", 5), ("E", 3),
    ("R", 2), ("R", 3), ("S", 1, 0, 1), ("C", 4), ("S", 1, 1, 2), ("C", 5), ("S", 1, 2, 4),
    ("E", 4), ("E", 5), ("R", 4), ("R", 5), ("S", 2, 0, 4),
)


def back_kernel(
    scale,
    root,
    routes_ref,
    weight_ref,
    hidden_ref,
    grad_ref,
    basis_g_ref,
    basis_h_ref,
    query_g_ref,
    query_h_ref,
    ids_ref,
    damp_ref,
    out_ref,
    corr_ref,
    basis_g,
    basis_h,
    token_hidden,
    token_grad,
    query_rows_g,
    query_rows_h,
    send_g,
    send_h,
    held_g,
    held_h,
    g_ref,
    h_ref,
    gsq,
    hsq,
    small,
    sums,
    corr,
    back,
    part,
    nearby,
    summed,
    far,
    inv,
    acc,
    ret_out,
    ret_in,
    basis_sem,
    dg_s,
    dg_r,
    dh_s,
    dh_r,
    small_s,
    small_r,
    ask_s,
    ask_r,
    core_s,
    core_r,
    rs_s,
    rs_r,
    ag_s,
    ag_r,
    cg_s,
    cg_r,
    ret_s,
    ret_r,
):
    e = lax.axis_index("expert")
    x = lax.axis_index("dp_0")
    z = lax.axis_index("dp_1")
    k = lax.axis_index("dp_2")
    xz = x * 2 + z
    chips = part.shape[2]
    experts = ret_out.shape[0]
    capacity = held_g.shape[1]
    rows, width_d = g_ref.shape
    width_ff = h_ref.shape[1]
    chunks = width_ff // CHUNK
    bf16, f32 = jnp.bfloat16, jnp.float32

    def dp_id(index):
        return {"dp_0": index // 4, "dp_1": lax.rem(index // 2, 2), "dp_2": lax.rem(index, 2)}

    def chip_id(index):
        return {"dp_0": index // 2, "dp_1": lax.rem(index, 2)}

    me = xz * 2 + k
    barrier = pltpu.get_barrier_semaphore()

    def greet_dp(d, _):
        pl.semaphore_signal(
            barrier, 1, device_id=dp_id(lax.rem(me + d, 2 * chips)), device_id_type=MESH
        )
        return 0

    def greet_expert(d, _):
        pl.semaphore_signal(
            barrier, 1, device_id={"expert": lax.rem(e + d, experts)}, device_id_type=MESH
        )
        return 0

    lax.fori_loop(1, 2 * chips, greet_dp, 0)
    lax.fori_loop(1, experts, greet_expert, 0)
    loads = [
        pltpu.make_async_copy(source, target, basis_sem.at[index])
        for index, (source, target) in enumerate(
            (
                (grad_ref, token_grad),
                (hidden_ref, token_hidden),
                (query_g_ref, query_rows_g),
                (query_h_ref, query_rows_h),
                (basis_h_ref, basis_h),
                (basis_g_ref, basis_g),
            )
        )
    ]
    for load in loads:
        load.start()

    def each(first, last, act):
        def once(d, _):
            act(d)
            return 0

        lax.fori_loop(first, last, once, 0)

    tokens = grad_ref.shape[0]
    top = routes_ref.shape[0]
    sent = tokens * top
    named = jnp.concatenate([routes_ref[j : j + 1, :] for j in range(top)], axis=1)
    onehot = (named == lax.broadcasted_iota(jnp.int32, (16, sent), 0)).astype(f32)

    def order_of(axis):
        index = lax.broadcasted_iota(jnp.int32, (sent, sent), axis)
        return jnp.where(index < tokens, index * top, (index - tokens) * top + 1)

    earlier = (order_of(0) < order_of(1)).astype(f32).astype(bf16)
    before = jnp.dot(onehot.astype(bf16), earlier, preferred_element_type=f32)
    within = jnp.sum(before * onehot, axis=0, keepdims=True).astype(jnp.int32)
    slots = named * capacity + within
    chosen = (slots == lax.broadcasted_iota(jnp.int32, (experts * capacity, sent), 0)).astype(f32)
    weights = jnp.concatenate([weight_ref[j : j + 1, :] for j in range(top)], axis=1)
    weight = jnp.sum(chosen * weights, axis=1, keepdims=True)
    picks = [chosen[:, j * tokens : (j + 1) * tokens].astype(bf16) for j in range(top)]
    loads[0].wait()
    gathered = jnp.dot(sum(picks[1:], picks[0]), token_grad[...], preferred_element_type=f32)
    send_g[...] = (weight * gathered).astype(bf16).reshape(send_g.shape)

    def dispatch_copy(source, target, ssem, rsem, d):
        to = lax.rem(e + d, experts)
        return pltpu.make_async_remote_copy(
            source.at[to],
            target.at[d],
            ssem.at[d],
            rsem.at[d],
            device_id={"expert": to},
            device_id_type=MESH,
        )

    def dg_copy(d):
        return dispatch_copy(send_g, held_g, dg_s, dg_r, d)

    def dh_copy(d):
        return dispatch_copy(send_h, held_h, dh_s, dh_r, d)

    pl.semaphore_wait(barrier, 2 * chips - 1 + experts - 1)
    each(1, experts, lambda d: dg_copy(d).start())
    loads[1].wait()
    hidden = token_hidden[...].astype(f32)
    moved = None
    for j in range(top):
        part_j = jnp.dot(picks[j], hidden[:, j, :].astype(bf16), preferred_element_type=f32)
        moved = part_j if moved is None else moved + part_j
    send_h[...] = moved.astype(bf16).reshape(send_h.shape)
    each(1, experts, lambda d: dh_copy(d).start())
    acc[...] = jnp.zeros_like(acc)
    back[...] = jnp.zeros_like(back)
    for j in range(experts):
        back[j, :capacity, :] = chosen[j * capacity : (j + 1) * capacity].astype(bf16)

    def rotate(value, basis, rotated, squared, first):
        turned = jnp.dot(value, basis[...], preferred_element_type=f32).astype(bf16)
        count = value.shape[0]
        rotated[first : first + count, :] = turned
        square = jnp.square(turned.astype(f32)).astype(bf16)
        squared[first : first + count, :] = square
        return jnp.sum(square.astype(f32), axis=1, keepdims=True)

    for load in loads[2:]:
        load.wait()
    row_g = [rotate(send_g[e], basis_g, g_ref, gsq, 0)]
    query_row = lax.broadcasted_iota(jnp.int32, (query_g_ref.shape[0], 1), 0) == ids_ref[0, 0]

    def query(ref, basis):
        turned = jnp.dot(ref[...], basis[...], preferred_element_type=f32)
        one = jnp.sum(jnp.where(query_row, turned, 0.0), axis=0, keepdims=True)
        return one.astype(bf16).astype(f32)

    query_g = query(query_rows_g, basis_g)
    query_h = query(query_rows_h, basis_h)
    for j in range(width_d // 128):
        small[k, x, z, j : j + 1, :] = query_g[:, j * 128 : (j + 1) * 128]
    for j in range(width_ff // 128):
        small[k, x, z, 16 + j : 17 + j, :] = query_h[:, j * 128 : (j + 1) * 128]

    def ask_near(half):
        return pltpu.make_async_remote_copy(
            small.at[k, x, half],
            small.at[k, x, half],
            ask_s.at[0],
            ask_r.at[0],
            device_id={"dp_1": 1 - z},
            device_id_type=MESH,
        )

    def ask_line(d, line):
        return pltpu.make_async_remote_copy(
            small.at[k, line],
            small.at[k, line],
            ask_s.at[d],
            ask_r.at[d],
            device_id={"dp_0": lax.rem(x + d, 4)},
            device_id_type=MESH,
        )

    def ask_core(side):
        return pltpu.make_async_remote_copy(
            small.at[side],
            small.at[side],
            ask_s.at[4],
            ask_r.at[4],
            device_id={"dp_2": 1 - k},
            device_id_type=MESH,
        )

    ask_near(z).start()
    for first, last in ((1, experts // 2), (experts // 2, experts)):
        each(first, last, lambda d: dg_copy(d).wait_recv())
        row_g.append(
            rotate(
                held_g[first:last].reshape((last - first) * capacity, width_d),
                basis_g,
                g_ref,
                gsq,
                first * capacity,
            )
        )
        if first == 1:
            ask_near(1 - z).wait_recv()
            each(1, 4, lambda d: ask_line(d, x).start())
        else:
            each(1, 4, lambda d: ask_line(d, lax.rem(x + 4 - d, 4)).wait_recv())
            ask_core(k).start()
    each(1, experts, lambda d: dh_copy(d).wait_recv())
    row_h = rotate(
        jnp.concatenate(
            [send_h[e], held_h[1:experts].reshape((experts - 1) * capacity, width_ff)], axis=0
        ),
        basis_h,
        h_ref,
        hsq,
        0,
    )

    def core_copy(c):
        return pltpu.make_async_remote_copy(
            part.at[c, 1 - k],
            nearby.at[c],
            core_s.at[c],
            core_r.at[c],
            device_id={"dp_2": 1 - k},
            device_id_type=MESH,
        )

    def rs_copy(c, d):
        to = lax.rem(xz + d, chips)
        return pltpu.make_async_remote_copy(
            summed.at[c, to],
            far.at[c, d],
            rs_s.at[c, d],
            rs_r.at[c, d],
            device_id=chip_id(to),
            device_id_type=MESH,
        )

    def ag_copy(c, d):
        to = lax.rem(xz + d, chips)
        return pltpu.make_async_remote_copy(
            inv.at[c, k, xz],
            inv.at[c, k, xz],
            ag_s.at[c, d],
            ag_r.at[c, d],
            device_id=chip_id(to),
            device_id_type=MESH,
        )

    def ag_arrival(c, d):
        origin = lax.rem(xz + chips - d, chips)
        return pltpu.make_async_remote_copy(
            inv.at[c, k, origin],
            inv.at[c, k, origin],
            ag_s.at[c, d],
            ag_r.at[c, d],
            device_id=chip_id(origin),
            device_id_type=MESH,
        )

    def cg_copy(c, side):
        return pltpu.make_async_remote_copy(
            inv.at[c, side],
            inv.at[c, side],
            cg_s.at[c],
            cg_r.at[c],
            device_id={"dp_2": 1 - k},
            device_id_type=MESH,
        )

    def small_copy(d, slot):
        return pltpu.make_async_remote_copy(
            sums.at[me],
            sums.at[slot],
            small_s.at[d],
            small_r.at[d],
            device_id=dp_id(lax.rem(me + d, 2 * chips)),
            device_id_type=MESH,
        )

    def spread(pair):
        both = lax.dot_general(
            hsq[:, pair * 2 * CHUNK : (pair + 1) * 2 * CHUNK],
            gsq[...],
            (((0,), (0,)), ((), ())),
            preferred_element_type=f32,
        ).astype(bf16)
        for half in range(2):
            for q in range(2 * chips):
                part[2 * pair + half, q % 2, q // 2] = both[
                    half * CHUNK : (half + 1) * CHUNK, q * CHUNK : (q + 1) * CHUNK
                ]
            core_copy(2 * pair + half).start()

    def share():
        own_sum = jnp.sum(jnp.concatenate(row_g, axis=0) * row_h, axis=0, keepdims=True)
        sums[me] = jnp.broadcast_to(own_sum, (8, 128))
        each(1, 2 * chips, lambda d: small_copy(d, me).start())

    def stage_one(c):
        core_copy(c).wait()
        summed[c] = (part[c, k].astype(f32) + nearby[c].astype(f32)).astype(bf16)
        each(1, chips, lambda d: rs_copy(c, d).start())

    def stage_two(c, level):
        each(1, chips, lambda d: rs_copy(c, d).wait_recv())
        total = summed[c, xz].astype(f32)
        for d in range(1, chips):
            total = total + far[c, d].astype(f32)
        block = total.T * scale
        corr[:, c * CHUNK : (c + 1) * CHUNK] = block
        inv[c, k, xz] = (1.0 / (block + level)).astype(bf16)
        each(1, chips, lambda d: ag_copy(c, d).start())

    def stage_three(c):
        each(1, chips, lambda d: ag_arrival(c, d).wait_recv())
        cg_copy(c, k).start()

    def ready(c):
        cg_copy(c, 1 - k).wait_recv()

    lane = lax.broadcasted_iota(jnp.int32, acc.shape, 1)
    group = 4

    def score(pair, first, last):
        def step(t, _):
            parts = []
            for j in range(group):
                pieces = []
                for q in range(2 * chips):
                    d = (q % chips) * 2 + q // chips
                    pieces.append(
                        g_ref[:, d * CHUNK : (d + 1) * CHUNK]
                        * small[j % 2, t, j // 2, d : d + 1, :].astype(bf16)
                    )
                parts.append(jnp.concatenate(pieces, axis=1))
            scaled = jnp.concatenate(parts, axis=0)
            weights = jnp.concatenate(
                [inv[2 * pair + half].reshape(width_d, CHUNK) for half in range(2)], axis=1
            )
            product = jnp.dot(scaled, weights, preferred_element_type=f32)
            total = acc[...]
            for j in range(group):
                n = t * group + j
                value = None
                for half in range(2):
                    c = 2 * pair + half
                    term = product[
                        j * rows : (j + 1) * rows, half * CHUNK : (half + 1) * CHUNK
                    ] * (
                        h_ref[:, c * CHUNK : (c + 1) * CHUNK].astype(f32)
                        * small[j % 2, t, j // 2, 16 + c : 17 + c, :]
                    )
                    value = term if value is None else value + term
                total = total + jnp.where(
                    lane == n, jnp.sum(value, axis=1, keepdims=True), 0.0
                )
            acc[...] = total
            return 0

        lax.fori_loop(first + z // 2, last + z // 2, step, 0)

    def small_arrival(d):
        small_copy(d, lax.rem(me + 2 * chips - d, 2 * chips)).wait_recv()

    spread(0)
    share()
    spread(1)
    stage_one(0)
    stage_one(1)
    spread(2)
    each(1, 2 * chips, small_arrival)
    complete = sums[0, 0:1, :]
    for n in range(1, 2 * chips):
        complete = complete + sums[n, 0:1, :]
    level = damp_ref[0] * (complete * (scale / (width_d * width_ff)) + eps)

    ask_core(1 - k).wait_recv()
    stages = {"A": stage_one, "C": lambda c: stage_two(c, level), "E": stage_three, "R": ready}
    for act, c, *span in ORDER:
        if act == "S":
            score(c, *span)
        else:
            stages[act](c)

    turned_scores = (acc[...] / root).T[: ret_out.shape[1], :]
    blank = jnp.zeros((ret_out.shape[1], 128 - capacity), f32)
    for d in range(experts):
        ret_out[d] = jnp.concatenate(
            [turned_scores[:, d * capacity : (d + 1) * capacity], blank], axis=1
        )

    def ret_copy(d, slot):
        return pltpu.make_async_remote_copy(
            ret_out.at[d],
            ret_in.at[slot],
            ret_s.at[d],
            ret_r.at[d],
            device_id={"expert": lax.rem(e + experts - d, experts)},
            device_id_type=MESH,
        )

    each(1, experts, lambda d: ret_copy(d, e).start())
    leave = pltpu.make_async_copy(corr, corr_ref, basis_sem.at[6])
    leave.start()
    ret_in[e] = ret_out[0]
    for c in range(chunks):
        each(1, chips, lambda d: rs_copy(c, d).wait_send())
        each(1, chips, lambda d: ag_copy(c, d).wait_send())
        cg_copy(c, k).wait_send()
    each(1, 2 * chips, lambda d: small_copy(d, me).wait_send())
    ask_near(z).wait_send()
    each(1, 4, lambda d: ask_line(d, x).wait_send())
    ask_core(k).wait_send()
    each(1, experts, lambda d: dg_copy(d).wait_send())
    each(1, experts, lambda d: dh_copy(d).wait_send())
    each(1, experts, lambda d: ret_copy(d, lax.rem(e + d, experts)).wait_recv())
    arrived = jnp.concatenate([ret_in[j] for j in range(experts)], axis=1)
    high = arrived.astype(bf16)
    rest = arrived - high.astype(f32)
    middle = rest.astype(bf16)
    low = (rest - middle.astype(f32)).astype(bf16)
    result = jnp.dot(
        jnp.concatenate([high, middle, low], axis=0),
        back[...].reshape(experts * 128, sent),
        preferred_element_type=f32,
    )
    queries = ret_out.shape[1]
    result = result[:queries] + result[queries : 2 * queries] + result[2 * queries :]
    for j in range(top):
        out_ref[j] = result[:, j * tokens : (j + 1) * tokens]
    each(1, experts, lambda d: ret_copy(d, e).wait_send())
    leave.wait()


def write_kernel(picked_ref, sums_ref, scores_ref, corr_ref, picked, sums, sems):
    pairs = ((sums_ref, sums, corr_ref), (picked_ref, picked, scores_ref))
    taken = [
        pltpu.make_async_copy(source, held, sems.at[0, i])
        for i, (source, held, _) in enumerate(pairs)
    ]
    put = [
        pltpu.make_async_copy(held, target, sems.at[1, i])
        for i, (_, held, target) in enumerate(pairs)
    ]
    for copy in taken:
        copy.start()
    for first, second in zip(taken, put):
        first.wait()
        second.start()
    for copy in put:
        copy.wait()


def body(
    token_hidden,
    token_grad,
    routes,
    route_weight,
    gradient_eigenbasis,
    basis_hidden,
    query_hidden,
    query_grad,
    query_ids,
    damping,
):
    experts = lax.axis_size("expert")
    replicas = lax.axis_size(DP)
    tokens, top, width_ff = token_hidden.shape
    width_d = token_grad.shape[1]
    capacity = tokens * top * 3 // (2 * experts)
    rows = experts * capacity
    chips = replicas // 2
    chunks = width_ff // CHUNK
    bf16, f32 = jnp.bfloat16, jnp.float32
    block = width_d // replicas
    dma = pltpu.SemaphoreType.DMA
    vmem = pl.BlockSpec(memory_space=pltpu.VMEM)
    anywhere = pl.BlockSpec(memory_space=pl.ANY)
    smem = pl.BlockSpec(memory_space=pltpu.SMEM)
    picked, corrections = pl.pallas_call(
        functools.partial(
            back_kernel, 1.0 / (replicas * experts * capacity), math.sqrt(width_d * width_ff)
        ),
        out_shape=(
            jax.ShapeDtypeStruct((top, replicas, tokens), f32),
            jax.ShapeDtypeStruct((block, width_ff), f32),
        ),
        in_specs=[vmem] * 2 + [anywhere] * 6 + [smem] * 2,
        out_specs=(vmem, anywhere),
        scratch_shapes=[
            pltpu.VMEM((width_d, width_d), bf16),
            pltpu.VMEM((width_ff, width_ff), bf16),
            pltpu.VMEM(token_hidden.shape, bf16),
            pltpu.VMEM(token_grad.shape, bf16),
            pltpu.VMEM(query_grad.shape[1:], bf16),
            pltpu.VMEM(query_hidden.shape[1:], bf16),
            pltpu.VMEM((experts, capacity, width_d), bf16),
            pltpu.VMEM((experts, capacity, width_ff), bf16),
            pltpu.VMEM((experts, capacity, width_d), bf16),
            pltpu.VMEM((experts, capacity, width_ff), bf16),
            pltpu.VMEM((rows, width_d), bf16),
            pltpu.VMEM((rows, width_ff), bf16),
            pltpu.VMEM((rows, width_d), bf16),
            pltpu.VMEM((rows, width_ff), bf16),
            pltpu.VMEM((2, chips // 2, 2, 24, 128), f32),
            pltpu.VMEM((replicas, 8, 128), f32),
            pltpu.VMEM((block, width_ff), f32),
            pltpu.VMEM((experts, 128, tokens * top), bf16),
            pltpu.VMEM((chunks, 2, chips, CHUNK, block), bf16),
            pltpu.VMEM((chunks, chips, CHUNK, block), bf16),
            pltpu.VMEM((chunks, chips, CHUNK, block), bf16),
            pltpu.VMEM((chunks, chips, CHUNK, block), bf16),
            pltpu.VMEM((chunks, 2, chips, block, CHUNK), bf16),
            pltpu.VMEM((rows, 128), f32),
            pltpu.VMEM((experts, replicas, 128), f32),
            pltpu.VMEM((experts, replicas, 128), f32),
            dma((7,)),
            dma((experts,)),
            dma((experts,)),
            dma((experts,)),
            dma((experts,)),
            dma((replicas,)),
            dma((replicas,)),
            dma((5,)),
            dma((5,)),
            dma((chunks,)),
            dma((chunks,)),
            dma((chunks, chips)),
            dma((chunks, chips)),
            dma((chunks, chips)),
            dma((chunks, chips)),
            dma((chunks,)),
            dma((chunks,)),
            dma((experts,)),
            dma((experts,)),
        ],
        compiler_params=pltpu.CompilerParams(
            collective_id=0, has_side_effects=True, vmem_limit_bytes=60 * 1024 * 1024
        ),
    )(
        routes.T,
        route_weight.T,
        token_hidden,
        token_grad,
        gradient_eigenbasis[0],
        basis_hidden[0],
        query_grad[0],
        query_hidden[0],
        query_ids,
        damping,
    )
    picked, corrections = pl.pallas_call(
        write_kernel,
        out_shape=tuple(jax.ShapeDtypeStruct(a.shape, f32) for a in (picked, corrections)),
        in_specs=[anywhere] * 2,
        out_specs=(anywhere, anywhere),
        scratch_shapes=[
            pltpu.VMEM(picked.shape, f32),
            pltpu.VMEM(corrections.shape, f32),
            dma((2, 2)),
        ],
        compiler_params=pltpu.CompilerParams(vmem_limit_bytes=60 * 1024 * 1024),
    )(picked, corrections)
    return (picked.transpose(2, 0, 1), corrections[None])


def solution(mesh):
    torus = Mesh(
        mesh.devices.reshape(mesh.shape["expert"], 4, 2, 2), ("expert", "dp_0", "dp_1", "dp_2")
    )
    placed = (
        P(EXPERT_DP, None, None),
        P(EXPERT_DP, None),
        P(EXPERT_DP, None),
        P(EXPERT_DP, None),
        P("expert", None, None),
        P("expert", None, None),
        P("expert", DP, None),
        P("expert", DP, None),
        P("expert", DP),
        P("expert"),
    )
    return jax.shard_map(
        body,
        mesh=torus,
        in_specs=placed,
        out_specs=(P(EXPERT_DP, None, None), P("expert", DP, None)),
        check_vma=False,
    )
```

```python
import functools
import math

import jax
import jax.numpy as jnp
from jax import lax
from jax.experimental import pallas as pl
from jax.experimental.pallas import tpu as pltpu
from jax.sharding import Mesh
from jax.sharding import PartitionSpec as P

DP = ("dp_0", "dp_1", "dp_2")
EXPERT_DP = ("expert", "dp_0", "dp_1", "dp_2")

eps = 1e-06


MESH = pl.DeviceIdType.MESH
WIDE = 256
ORDER = (
    ("C", 0), ("A", 2), ("C", 1), ("A", 3), ("E", 0), ("R", 0), ("S", 0, 0, 2), ("C", 2), ("A", 4),
    ("S", 0, 2, 3), ("E", 1), ("S", 0, 3, 4), ("R", 1), ("S", 1, 0, 2), ("C", 3), ("A", 5),
    ("S", 1, 2, 3), ("E", 2), ("S", 1, 3, 4), ("R", 2), ("S", 2, 0, 2), ("C", 4), ("S", 2, 2, 3),
    ("E", 3), ("S", 2, 3, 4), ("R", 3), ("S", 3, 0, 2), ("C", 5), ("S", 3, 2, 3), ("E", 4),
    ("S", 3, 3, 4), ("R", 4), ("S", 4, 0, 2), ("E", 5), ("S", 4, 2, 4), ("R", 5), ("S", 5, 0, 4),
)


def pair_of(tile, chips):
    return tuple((q % chips) * 2 + q // chips for q in (2 * tile, 2 * tile + 1))


def back_kernel(
    scale,
    root,
    routes_ref,
    weight_ref,
    hidden_ref,
    grad_ref,
    basis_g_ref,
    basis_h_ref,
    query_g_ref,
    query_h_ref,
    ids_ref,
    damp_ref,
    out_ref,
    corr_ref,
    basis_g,
    basis_h,
    token_hidden,
    token_grad,
    query_rows_g,
    query_rows_h,
    send_g,
    send_h,
    held_g,
    held_h,
    g_ref,
    h_ref,
    gsq,
    hsq,
    small,
    sums,
    corr,
    ordered,
    back,
    part,
    nearby,
    summed,
    far,
    inv,
    acc,
    ret_out,
    ret_in,
    basis_sem,
    dg_s,
    dg_r,
    dh_s,
    dh_r,
    small_s,
    small_r,
    ask_s,
    ask_r,
    core_s,
    core_r,
    rs_s,
    rs_r,
    ag_s,
    ag_r,
    cg_s,
    cg_r,
    ret_s,
    ret_r,
):
    e = lax.axis_index("expert")
    x = lax.axis_index("dp_0")
    z = lax.axis_index("dp_1")
    k = lax.axis_index("dp_2")
    xz = x * 2 + z
    chips = part.shape[2]
    experts = ret_out.shape[0]
    capacity = held_g.shape[1]
    rows, width_d = g_ref.shape
    width_ff = h_ref.shape[1]
    chunks = part.shape[0]
    half_rows = part.shape[3]
    bf16, f32 = jnp.bfloat16, jnp.float32

    def halves(row, unit_half, tile):
        return jnp.concatenate(
            [
                row[:, d * 128 + unit_half * half_rows : d * 128 + (unit_half + 1) * half_rows]
                for d in pair_of(tile, chips)
            ],
            axis=1,
        )

    def dp_id(index):
        return {"dp_0": index // 4, "dp_1": lax.rem(index // 2, 2), "dp_2": lax.rem(index, 2)}

    def chip_id(index):
        return {"dp_0": index // 2, "dp_1": lax.rem(index, 2)}

    me = xz * 2 + k
    barrier = pltpu.get_barrier_semaphore()

    def greet_dp(d, _):
        pl.semaphore_signal(
            barrier, 1, device_id=dp_id(lax.rem(me + d, 2 * chips)), device_id_type=MESH
        )
        return 0

    def greet_expert(d, _):
        pl.semaphore_signal(
            barrier, 1, device_id={"expert": lax.rem(e + d, experts)}, device_id_type=MESH
        )
        return 0

    lax.fori_loop(1, 2 * chips, greet_dp, 0)
    lax.fori_loop(1, experts, greet_expert, 0)
    loads = [
        pltpu.make_async_copy(source, target, basis_sem.at[index])
        for index, (source, target) in enumerate(
            (
                (grad_ref, token_grad),
                (hidden_ref, token_hidden),
                (query_g_ref, query_rows_g),
                (query_h_ref, query_rows_h),
                (basis_h_ref, basis_h),
                (basis_g_ref, basis_g),
            )
        )
    ]
    for load in loads:
        load.start()

    def each(first, last, act):
        def once(d, _):
            act(d)
            return 0

        lax.fori_loop(first, last, once, 0)

    tokens = grad_ref.shape[0]
    top = routes_ref.shape[0]
    sent = tokens * top
    named = jnp.concatenate([routes_ref[j : j + 1, :] for j in range(top)], axis=1)
    onehot = (named == lax.broadcasted_iota(jnp.int32, (16, sent), 0)).astype(f32)

    def order_of(axis):
        index = lax.broadcasted_iota(jnp.int32, (sent, sent), axis)
        return jnp.where(index < tokens, index * top, (index - tokens) * top + 1)

    earlier = (order_of(0) < order_of(1)).astype(f32).astype(bf16)
    before = jnp.dot(onehot.astype(bf16), earlier, preferred_element_type=f32)
    within = jnp.sum(before * onehot, axis=0, keepdims=True).astype(jnp.int32)
    slots = named * capacity + within
    chosen = (slots == lax.broadcasted_iota(jnp.int32, (experts * capacity, sent), 0)).astype(f32)
    weights = jnp.concatenate([weight_ref[j : j + 1, :] for j in range(top)], axis=1)
    weight = jnp.sum(chosen * weights, axis=1, keepdims=True)
    picks = [chosen[:, j * tokens : (j + 1) * tokens].astype(bf16) for j in range(top)]
    loads[0].wait()
    gathered = jnp.dot(sum(picks[1:], picks[0]), token_grad[...], preferred_element_type=f32)
    send_g[...] = (weight * gathered).astype(bf16).reshape(send_g.shape)

    def dispatch_copy(source, target, ssem, rsem, d):
        to = lax.rem(e + d, experts)
        return pltpu.make_async_remote_copy(
            source.at[to],
            target.at[d],
            ssem.at[d],
            rsem.at[d],
            device_id={"expert": to},
            device_id_type=MESH,
        )

    def dg_copy(d):
        return dispatch_copy(send_g, held_g, dg_s, dg_r, d)

    def dh_copy(d):
        return dispatch_copy(send_h, held_h, dh_s, dh_r, d)

    pl.semaphore_wait(barrier, 2 * chips - 1 + experts - 1)
    each(1, experts, lambda d: dg_copy(d).start())
    loads[1].wait()
    hidden = token_hidden[...].astype(f32)
    moved = None
    for j in range(top):
        part_j = jnp.dot(picks[j], hidden[:, j, :].astype(bf16), preferred_element_type=f32)
        moved = part_j if moved is None else moved + part_j
    send_h[...] = moved.astype(bf16).reshape(send_h.shape)
    each(1, experts, lambda d: dh_copy(d).start())
    acc[...] = jnp.zeros_like(acc)
    back[...] = jnp.zeros_like(back)
    for j in range(experts):
        back[j, :capacity, :] = chosen[j * capacity : (j + 1) * capacity].astype(bf16)

    def rotate(value, basis, rotated, squared, first):
        turned = jnp.dot(value, basis[...], preferred_element_type=f32).astype(bf16)
        count = value.shape[0]
        rotated[first : first + count, :] = turned
        square = jnp.square(turned.astype(f32)).astype(bf16)
        squared[first : first + count, :] = square
        return jnp.sum(square.astype(f32), axis=1, keepdims=True)

    for load in loads[2:]:
        load.wait()
    row_g = [rotate(send_g[e], basis_g, g_ref, gsq, 0)]
    query_row = lax.broadcasted_iota(jnp.int32, (query_g_ref.shape[0], 1), 0) == ids_ref[0, 0]

    def query(ref, basis):
        turned = jnp.dot(ref[...], basis[...], preferred_element_type=f32)
        one = jnp.sum(jnp.where(query_row, turned, 0.0), axis=0, keepdims=True)
        return one.astype(bf16).astype(f32)

    query_g = query(query_rows_g, basis_g)
    query_h = query(query_rows_h, basis_h)
    for j in range(width_d // 128):
        small[k, x, z, j : j + 1, :] = halves(query_g, j // chips, j % chips)
    for j in range(width_ff // 128):
        small[k, x, z, 16 + j : 17 + j, :] = query_h[:, j * 128 : (j + 1) * 128]

    def ask_near(half):
        return pltpu.make_async_remote_copy(
            small.at[k, x, half],
            small.at[k, x, half],
            ask_s.at[0],
            ask_r.at[0],
            device_id={"dp_1": 1 - z},
            device_id_type=MESH,
        )

    def ask_line(d, line):
        return pltpu.make_async_remote_copy(
            small.at[k, line],
            small.at[k, line],
            ask_s.at[d],
            ask_r.at[d],
            device_id={"dp_0": lax.rem(x + d, 4)},
            device_id_type=MESH,
        )

    def ask_core(side):
        return pltpu.make_async_remote_copy(
            small.at[side],
            small.at[side],
            ask_s.at[4],
            ask_r.at[4],
            device_id={"dp_2": 1 - k},
            device_id_type=MESH,
        )

    ask_near(z).start()
    for first, last in ((1, experts // 2), (experts // 2, experts)):
        each(first, last, lambda d: dg_copy(d).wait_recv())
        row_g.append(
            rotate(
                held_g[first:last].reshape((last - first) * capacity, width_d),
                basis_g,
                g_ref,
                gsq,
                first * capacity,
            )
        )
        if first == 1:
            ask_near(1 - z).wait_recv()
            each(1, 4, lambda d: ask_line(d, x).start())
        else:
            each(1, 4, lambda d: ask_line(d, lax.rem(x + 4 - d, 4)).wait_recv())
            ask_core(k).start()
    each(1, experts, lambda d: dh_copy(d).wait_recv())
    row_h = rotate(
        jnp.concatenate(
            [send_h[e], held_h[1:experts].reshape((experts - 1) * capacity, width_ff)], axis=0
        ),
        basis_h,
        h_ref,
        hsq,
        0,
    )

    def core_copy(c):
        return pltpu.make_async_remote_copy(
            part.at[c, 1 - k],
            nearby.at[c],
            core_s.at[c],
            core_r.at[c],
            device_id={"dp_2": 1 - k},
            device_id_type=MESH,
        )

    def rs_copy(c, d):
        to = lax.rem(xz + d, chips)
        return pltpu.make_async_remote_copy(
            summed.at[c, to],
            far.at[c, d],
            rs_s.at[c, d],
            rs_r.at[c, d],
            device_id=chip_id(to),
            device_id_type=MESH,
        )

    def ag_copy(c, d):
        to = lax.rem(xz + d, chips)
        return pltpu.make_async_remote_copy(
            inv.at[c, k, xz],
            inv.at[c, k, xz],
            ag_s.at[c, d],
            ag_r.at[c, d],
            device_id=chip_id(to),
            device_id_type=MESH,
        )

    def ag_arrival(c, d):
        origin = lax.rem(xz + chips - d, chips)
        return pltpu.make_async_remote_copy(
            inv.at[c, k, origin],
            inv.at[c, k, origin],
            ag_s.at[c, d],
            ag_r.at[c, d],
            device_id=chip_id(origin),
            device_id_type=MESH,
        )

    def cg_copy(c, side):
        return pltpu.make_async_remote_copy(
            inv.at[c, side],
            inv.at[c, side],
            cg_s.at[c],
            cg_r.at[c],
            device_id={"dp_2": 1 - k},
            device_id_type=MESH,
        )

    def small_copy(d, slot):
        return pltpu.make_async_remote_copy(
            sums.at[me],
            sums.at[slot],
            small_s.at[d],
            small_r.at[d],
            device_id=dp_id(lax.rem(me + d, 2 * chips)),
            device_id_type=MESH,
        )

    def spread(pair):
        both = lax.dot_general(
            gsq[...],
            hsq[:, pair * WIDE : (pair + 1) * WIDE],
            (((0,), (0,)), ((), ())),
            preferred_element_type=f32,
        ).astype(bf16)
        for half in range(2):
            for q in range(2 * chips):
                first = q * 128 + half * half_rows
                part[2 * pair + half, q % 2, q // 2] = both[first : first + half_rows, :]
            core_copy(2 * pair + half).start()

    def share():
        own_sum = jnp.sum(jnp.concatenate(row_g, axis=0) * row_h, axis=0, keepdims=True)
        sums[me] = jnp.broadcast_to(own_sum, (8, 128))
        each(1, 2 * chips, lambda d: small_copy(d, me).start())

    def stage_one(c):
        core_copy(c).wait()
        summed[c] = (part[c, k].astype(f32) + nearby[c].astype(f32)).astype(bf16)
        each(1, chips, lambda d: rs_copy(c, d).start())

    def stage_two(c, level):
        each(1, chips, lambda d: rs_copy(c, d).wait_recv())
        total = summed[c, xz].astype(f32)
        for d in range(1, chips):
            total = total + far[c, d].astype(f32)
        block = total * scale
        first, left = (c % 2) * half_rows, (c // 2) * WIDE
        corr[first : first + half_rows, left : left + WIDE] = block
        inv[c, k, xz] = (1.0 / (block + level)).astype(bf16)
        each(1, chips, lambda d: ag_copy(c, d).start())

    def stage_three(c):
        each(1, chips, lambda d: ag_arrival(c, d).wait_recv())
        cg_copy(c, k).start()

    def ready(c):
        cg_copy(c, 1 - k).wait_recv()

    lane = lax.broadcasted_iota(jnp.int32, acc.shape, 1)
    group = 4

    def score(unit, first, last):
        left = (unit // 2) * WIDE

        def step(t, _):
            parts = []
            for j in range(group):
                pieces = []
                for tile in range(chips):
                    row = (unit % 2) * chips + tile
                    pieces.append(
                        ordered[unit % 2, :, tile * 128 : (tile + 1) * 128]
                        * small[j % 2, t, j // 2, row : row + 1, :].astype(bf16)
                    )
                parts.append(jnp.concatenate(pieces, axis=1))
            scaled = jnp.concatenate(parts, axis=0)
            weights = inv[unit].reshape(width_d // 2, WIDE)
            product = jnp.dot(scaled, weights, preferred_element_type=f32)
            total = acc[...]
            for j in range(group):
                n = t * group + j
                value = None
                for side in range(WIDE // 128):
                    c = left // 128 + side
                    term = product[
                        j * rows : (j + 1) * rows, side * 128 : (side + 1) * 128
                    ] * (
                        h_ref[:, c * 128 : (c + 1) * 128].astype(f32)
                        * small[j % 2, t, j // 2, 16 + c : 17 + c, :]
                    )
                    value = term if value is None else value + term
                total = total + jnp.where(
                    lane == n, jnp.sum(value, axis=1, keepdims=True), 0.0
                )
            acc[...] = total
            return 0

        lax.fori_loop(first + z // 2, last + z // 2, step, 0)

    def small_arrival(d):
        small_copy(d, lax.rem(me + 2 * chips - d, 2 * chips)).wait_recv()

    spread(0)
    share()
    spread(1)
    stage_one(0)
    stage_one(1)
    spread(2)
    for half in range(2):
        for tile in range(chips):
            ordered[half, :, tile * 128 : (tile + 1) * 128] = halves(g_ref, half, tile)
    each(1, 2 * chips, small_arrival)
    complete = sums[0, 0:1, :]
    for n in range(1, 2 * chips):
        complete = complete + sums[n, 0:1, :]
    level = damp_ref[0] * (complete * (scale / (width_d * width_ff)) + eps)
    level = jnp.concatenate([level] * (WIDE // 128), axis=1)

    ask_core(1 - k).wait_recv()
    stages = {"A": stage_one, "C": lambda c: stage_two(c, level), "E": stage_three, "R": ready}
    for act, c, *span in ORDER:
        if act == "S":
            score(c, *span)
        else:
            stages[act](c)

    turned_scores = (acc[...] / root).T[: ret_out.shape[1], :]
    blank = jnp.zeros((ret_out.shape[1], 128 - capacity), f32)
    for d in range(experts):
        ret_out[d] = jnp.concatenate(
            [turned_scores[:, d * capacity : (d + 1) * capacity], blank], axis=1
        )

    def ret_copy(d, slot):
        return pltpu.make_async_remote_copy(
            ret_out.at[d],
            ret_in.at[slot],
            ret_s.at[d],
            ret_r.at[d],
            device_id={"expert": lax.rem(e + experts - d, experts)},
            device_id_type=MESH,
        )

    each(1, experts, lambda d: ret_copy(d, e).start())
    leave = pltpu.make_async_copy(corr, corr_ref, basis_sem.at[6])
    leave.start()
    ret_in[e] = ret_out[0]
    for c in range(chunks):
        each(1, chips, lambda d: rs_copy(c, d).wait_send())
        each(1, chips, lambda d: ag_copy(c, d).wait_send())
        cg_copy(c, k).wait_send()
    each(1, 2 * chips, lambda d: small_copy(d, me).wait_send())
    ask_near(z).wait_send()
    each(1, 4, lambda d: ask_line(d, x).wait_send())
    ask_core(k).wait_send()
    each(1, experts, lambda d: dg_copy(d).wait_send())
    each(1, experts, lambda d: dh_copy(d).wait_send())
    each(1, experts, lambda d: ret_copy(d, lax.rem(e + d, experts)).wait_recv())
    arrived = jnp.concatenate([ret_in[j] for j in range(experts)], axis=1)
    high = arrived.astype(bf16)
    rest = arrived - high.astype(f32)
    middle = rest.astype(bf16)
    low = (rest - middle.astype(f32)).astype(bf16)
    result = jnp.dot(
        jnp.concatenate([high, middle, low], axis=0),
        back[...].reshape(experts * 128, sent),
        preferred_element_type=f32,
    )
    queries = ret_out.shape[1]
    result = result[:queries] + result[queries : 2 * queries] + result[2 * queries :]
    for j in range(top):
        out_ref[j] = result[:, j * tokens : (j + 1) * tokens]
    each(1, experts, lambda d: ret_copy(d, e).wait_send())
    leave.wait()


def write_kernel(picked_ref, sums_ref, scores_ref, corr_ref, picked, sums, sems):
    pairs = ((sums_ref, sums, corr_ref), (picked_ref, picked, scores_ref))
    taken = [
        pltpu.make_async_copy(source, held, sems.at[0, i])
        for i, (source, held, _) in enumerate(pairs)
    ]
    put = [
        pltpu.make_async_copy(held, target, sems.at[1, i])
        for i, (_, held, target) in enumerate(pairs)
    ]
    for copy in taken:
        copy.start()
    for first, second in zip(taken, put):
        first.wait()
        second.start()
    for copy in put:
        copy.wait()


def body(
    token_hidden,
    token_grad,
    routes,
    route_weight,
    gradient_eigenbasis,
    basis_hidden,
    query_hidden,
    query_grad,
    query_ids,
    damping,
):
    experts = lax.axis_size("expert")
    replicas = lax.axis_size(DP)
    tokens, top, width_ff = token_hidden.shape
    width_d = token_grad.shape[1]
    capacity = tokens * top * 3 // (2 * experts)
    rows = experts * capacity
    chips = replicas // 2
    chunks = 2 * width_ff // WIDE
    bf16, f32 = jnp.bfloat16, jnp.float32
    block = width_d // replicas
    dma = pltpu.SemaphoreType.DMA
    vmem = pl.BlockSpec(memory_space=pltpu.VMEM)
    anywhere = pl.BlockSpec(memory_space=pl.ANY)
    smem = pl.BlockSpec(memory_space=pltpu.SMEM)
    picked, corrections = pl.pallas_call(
        functools.partial(
            back_kernel, 1.0 / (replicas * experts * capacity), math.sqrt(width_d * width_ff)
        ),
        out_shape=(
            jax.ShapeDtypeStruct((top, replicas, tokens), f32),
            jax.ShapeDtypeStruct((block, width_ff), f32),
        ),
        in_specs=[vmem] * 2 + [anywhere] * 6 + [smem] * 2,
        out_specs=(vmem, anywhere),
        scratch_shapes=[
            pltpu.VMEM((width_d, width_d), bf16),
            pltpu.VMEM((width_ff, width_ff), bf16),
            pltpu.VMEM(token_hidden.shape, bf16),
            pltpu.VMEM(token_grad.shape, bf16),
            pltpu.VMEM(query_grad.shape[1:], bf16),
            pltpu.VMEM(query_hidden.shape[1:], bf16),
            pltpu.VMEM((experts, capacity, width_d), bf16),
            pltpu.VMEM((experts, capacity, width_ff), bf16),
            pltpu.VMEM((experts, capacity, width_d), bf16),
            pltpu.VMEM((experts, capacity, width_ff), bf16),
            pltpu.VMEM((rows, width_d), bf16),
            pltpu.VMEM((rows, width_ff), bf16),
            pltpu.VMEM((rows, width_d), bf16),
            pltpu.VMEM((rows, width_ff), bf16),
            pltpu.VMEM((2, chips // 2, 2, 24, 128), f32),
            pltpu.VMEM((replicas, 8, 128), f32),
            pltpu.VMEM((block, width_ff), f32),
            pltpu.VMEM((2, rows, width_d // 2), bf16),
            pltpu.VMEM((experts, 128, tokens * top), bf16),
            pltpu.VMEM((chunks, 2, chips, block // 2, WIDE), bf16),
            pltpu.VMEM((chunks, chips, block // 2, WIDE), bf16),
            pltpu.VMEM((chunks, chips, block // 2, WIDE), bf16),
            pltpu.VMEM((chunks, chips, block // 2, WIDE), bf16),
            pltpu.VMEM((chunks, 2, chips, block // 2, WIDE), bf16),
            pltpu.VMEM((rows, 128), f32),
            pltpu.VMEM((experts, replicas, 128), f32),
            pltpu.VMEM((experts, replicas, 128), f32),
            dma((7,)),
            dma((experts,)),
            dma((experts,)),
            dma((experts,)),
            dma((experts,)),
            dma((replicas,)),
            dma((replicas,)),
            dma((5,)),
            dma((5,)),
            dma((chunks,)),
            dma((chunks,)),
            dma((chunks, chips)),
            dma((chunks, chips)),
            dma((chunks, chips)),
            dma((chunks, chips)),
            dma((chunks,)),
            dma((chunks,)),
            dma((experts,)),
            dma((experts,)),
        ],
        compiler_params=pltpu.CompilerParams(
            collective_id=0, has_side_effects=True, vmem_limit_bytes=60 * 1024 * 1024
        ),
    )(
        routes.T,
        route_weight.T,
        token_hidden,
        token_grad,
        gradient_eigenbasis[0],
        basis_hidden[0],
        query_grad[0],
        query_hidden[0],
        query_ids,
        damping,
    )
    picked, corrections = pl.pallas_call(
        write_kernel,
        out_shape=tuple(jax.ShapeDtypeStruct(a.shape, f32) for a in (picked, corrections)),
        in_specs=[anywhere] * 2,
        out_specs=(anywhere, anywhere),
        scratch_shapes=[
            pltpu.VMEM(picked.shape, f32),
            pltpu.VMEM(corrections.shape, f32),
            dma((2, 2)),
        ],
        compiler_params=pltpu.CompilerParams(vmem_limit_bytes=60 * 1024 * 1024),
    )(picked, corrections)
    return (picked.transpose(2, 0, 1), corrections[None])


def solution(mesh):
    torus = Mesh(
        mesh.devices.reshape(mesh.shape["expert"], 4, 2, 2), ("expert", "dp_0", "dp_1", "dp_2")
    )
    placed = (
        P(EXPERT_DP, None, None),
        P(EXPERT_DP, None),
        P(EXPERT_DP, None),
        P(EXPERT_DP, None),
        P("expert", None, None),
        P("expert", None, None),
        P("expert", DP, None),
        P("expert", DP, None),
        P("expert", DP),
        P("expert"),
    )
    return jax.shard_map(
        body,
        mesh=torus,
        in_specs=placed,
        out_specs=(P(EXPERT_DP, None, None), P("expert", DP, None)),
        check_vma=False,
    )
```

```python
import functools
import math

import jax
import jax.numpy as jnp
from jax import lax
from jax.experimental import pallas as pl
from jax.experimental.pallas import tpu as pltpu
from jax.sharding import Mesh
from jax.sharding import PartitionSpec as P

DP = ("dp_0", "dp_1", "dp_2")
EXPERT_DP = ("expert", "dp_0", "dp_1", "dp_2")

eps = 1e-06


MESH = pl.DeviceIdType.MESH
WIDE = 256
ORDER = (
    ("C", 0), ("A", 2), ("C", 1), ("A", 3), ("E", 0), ("R", 0), ("S", 0, 0, 2), ("C", 2), ("A", 4),
    ("S", 0, 2, 3), ("E", 1), ("S", 0, 3, 4), ("R", 1), ("S", 1, 0, 2), ("C", 3), ("A", 5),
    ("S", 1, 2, 3), ("E", 2), ("S", 1, 3, 4), ("R", 2), ("S", 2, 0, 2), ("C", 4), ("S", 2, 2, 3),
    ("E", 3), ("S", 2, 3, 4), ("R", 3), ("S", 3, 0, 2), ("C", 5), ("S", 3, 2, 3), ("E", 4),
    ("S", 3, 3, 4), ("R", 4), ("S", 4, 0, 2), ("E", 5), ("S", 4, 2, 4), ("R", 5), ("S", 5, 0, 4),
)


def pair_of(tile, chips):
    return tuple((q % chips) * 2 + q // chips for q in (2 * tile, 2 * tile + 1))


def back_kernel(
    scale,
    root,
    routes_ref,
    weight_ref,
    hidden_ref,
    grad_ref,
    basis_g_ref,
    basis_h_ref,
    query_g_ref,
    query_h_ref,
    ids_ref,
    damp_ref,
    out_ref,
    corr_ref,
    basis_g,
    basis_h,
    token_hidden,
    token_grad,
    query_rows_g,
    query_rows_h,
    send_g,
    send_h,
    held_g,
    held_h,
    g_ref,
    h_ref,
    gsq,
    hsq,
    small,
    sums,
    corr,
    ordered,
    back,
    part,
    nearby,
    summed,
    far,
    inv,
    acc,
    ret_out,
    ret_in,
    basis_sem,
    dg_s,
    dg_r,
    dh_s,
    dh_r,
    small_s,
    small_r,
    ask_s,
    ask_r,
    core_s,
    core_r,
    rs_s,
    rs_r,
    ag_s,
    ag_r,
    cg_s,
    cg_r,
    ret_s,
    ret_r,
):
    e = lax.axis_index("expert")
    x = lax.axis_index("dp_0")
    z = lax.axis_index("dp_1")
    k = lax.axis_index("dp_2")
    xz = x * 2 + z
    chips = part.shape[2]
    experts = ret_out.shape[0]
    capacity = held_g.shape[1]
    rows, width_d = g_ref.shape
    width_ff = h_ref.shape[1]
    chunks = part.shape[0]
    half_rows = part.shape[3]
    bf16, f32 = jnp.bfloat16, jnp.float32

    def halves(row, unit_half, tile):
        return jnp.concatenate(
            [
                row[:, d * 128 + unit_half * half_rows : d * 128 + (unit_half + 1) * half_rows]
                for d in pair_of(tile, chips)
            ],
            axis=1,
        )

    def dp_id(index):
        return {"dp_0": index // 4, "dp_1": lax.rem(index // 2, 2), "dp_2": lax.rem(index, 2)}

    def chip_id(index):
        return {"dp_0": index // 2, "dp_1": lax.rem(index, 2)}

    me = xz * 2 + k
    barrier = pltpu.get_barrier_semaphore()

    def greet_dp(d, _):
        pl.semaphore_signal(
            barrier, 1, device_id=dp_id(lax.rem(me + d, 2 * chips)), device_id_type=MESH
        )
        return 0

    def greet_expert(d, _):
        pl.semaphore_signal(
            barrier, 1, device_id={"expert": lax.rem(e + d, experts)}, device_id_type=MESH
        )
        return 0

    lax.fori_loop(1, 2 * chips, greet_dp, 0)
    lax.fori_loop(1, experts, greet_expert, 0)
    loads = [
        pltpu.make_async_copy(source, target, basis_sem.at[index])
        for index, (source, target) in enumerate(
            (
                (grad_ref, token_grad),
                (hidden_ref, token_hidden),
                (query_g_ref, query_rows_g),
                (query_h_ref, query_rows_h),
                (basis_h_ref, basis_h),
                (basis_g_ref, basis_g),
            )
        )
    ]
    for load in loads:
        load.start()

    def each(first, last, act):
        def once(d, _):
            act(d)
            return 0

        lax.fori_loop(first, last, once, 0)

    tokens = grad_ref.shape[0]
    top = routes_ref.shape[0]
    sent = tokens * top
    named = jnp.concatenate([routes_ref[j : j + 1, :] for j in range(top)], axis=1)
    onehot = (named == lax.broadcasted_iota(jnp.int32, (16, sent), 0)).astype(f32)

    def order_of(axis):
        index = lax.broadcasted_iota(jnp.int32, (sent, sent), axis)
        return jnp.where(index < tokens, index * top, (index - tokens) * top + 1)

    earlier = (order_of(0) < order_of(1)).astype(f32).astype(bf16)
    before = jnp.dot(onehot.astype(bf16), earlier, preferred_element_type=f32)
    within = jnp.sum(before * onehot, axis=0, keepdims=True).astype(jnp.int32)
    slots = named * capacity + within
    chosen = (slots == lax.broadcasted_iota(jnp.int32, (experts * capacity, sent), 0)).astype(f32)
    weights = jnp.concatenate([weight_ref[j : j + 1, :] for j in range(top)], axis=1)
    weight = jnp.sum(chosen * weights, axis=1, keepdims=True)
    picks = [chosen[:, j * tokens : (j + 1) * tokens].astype(bf16) for j in range(top)]
    loads[0].wait()
    gathered = jnp.dot(sum(picks[1:], picks[0]), token_grad[...], preferred_element_type=f32)
    send_g[...] = (weight * gathered).astype(bf16).reshape(send_g.shape)

    def dispatch_copy(source, target, ssem, rsem, d):
        to = lax.rem(e + d, experts)
        return pltpu.make_async_remote_copy(
            source.at[to],
            target.at[d],
            ssem.at[d],
            rsem.at[d],
            device_id={"expert": to},
            device_id_type=MESH,
        )

    def dg_copy(d):
        return dispatch_copy(send_g, held_g, dg_s, dg_r, d)

    def dh_copy(d):
        return dispatch_copy(send_h, held_h, dh_s, dh_r, d)

    pl.semaphore_wait(barrier, 2 * chips - 1 + experts - 1)
    each(1, experts, lambda d: dg_copy(d).start())
    loads[1].wait()
    hidden = token_hidden[...].astype(f32)
    moved = None
    for j in range(top):
        part_j = jnp.dot(picks[j], hidden[:, j, :].astype(bf16), preferred_element_type=f32)
        moved = part_j if moved is None else moved + part_j
    send_h[...] = moved.astype(bf16).reshape(send_h.shape)
    each(1, experts, lambda d: dh_copy(d).start())
    acc[...] = jnp.zeros_like(acc)
    back[...] = jnp.zeros_like(back)
    for j in range(experts):
        back[j, :capacity, :] = chosen[j * capacity : (j + 1) * capacity].astype(bf16)

    def rotate(value, basis, rotated, squared, first):
        turned = jnp.dot(value, basis[...], preferred_element_type=f32).astype(bf16)
        count = value.shape[0]
        rotated[first : first + count, :] = turned
        square = jnp.square(turned.astype(f32)).astype(bf16)
        squared[first : first + count, :] = square
        return jnp.sum(square.astype(f32), axis=1, keepdims=True)

    for load in loads[2:]:
        load.wait()
    row_g = [rotate(send_g[e], basis_g, g_ref, gsq, 0)]
    query_row = lax.broadcasted_iota(jnp.int32, (query_g_ref.shape[0], 1), 0) == ids_ref[0, 0]

    def query(ref, basis):
        turned = jnp.dot(ref[...], basis[...], preferred_element_type=f32)
        one = jnp.sum(jnp.where(query_row, turned, 0.0), axis=0, keepdims=True)
        return one.astype(bf16).astype(f32)

    query_g = query(query_rows_g, basis_g)
    query_h = query(query_rows_h, basis_h)
    for j in range(width_d // 128):
        small[k, x, z, j : j + 1, :] = halves(query_g, j // chips, j % chips)
    for j in range(width_ff // 128):
        small[k, x, z, 16 + j : 17 + j, :] = query_h[:, j * 128 : (j + 1) * 128]

    def ask_near(half):
        return pltpu.make_async_remote_copy(
            small.at[k, x, half],
            small.at[k, x, half],
            ask_s.at[0],
            ask_r.at[0],
            device_id={"dp_1": 1 - z},
            device_id_type=MESH,
        )

    def ask_line(d, line):
        return pltpu.make_async_remote_copy(
            small.at[k, line],
            small.at[k, line],
            ask_s.at[d],
            ask_r.at[d],
            device_id={"dp_0": lax.rem(x + d, 4)},
            device_id_type=MESH,
        )

    def ask_core(side):
        return pltpu.make_async_remote_copy(
            small.at[side],
            small.at[side],
            ask_s.at[4],
            ask_r.at[4],
            device_id={"dp_2": 1 - k},
            device_id_type=MESH,
        )

    ask_near(z).start()
    for first, last in ((1, experts // 2), (experts // 2, experts)):
        each(first, last, lambda d: dg_copy(d).wait_recv())
        row_g.append(
            rotate(
                held_g[first:last].reshape((last - first) * capacity, width_d),
                basis_g,
                g_ref,
                gsq,
                first * capacity,
            )
        )
        if first == 1:
            ask_near(1 - z).wait_recv()
            each(1, 4, lambda d: ask_line(d, x).start())
        else:
            each(1, 4, lambda d: ask_line(d, lax.rem(x + 4 - d, 4)).wait_recv())
            ask_core(k).start()
    each(1, experts, lambda d: dh_copy(d).wait_recv())

    def rotate_hidden(left, right):
        value = jnp.concatenate(
            [send_h[e], held_h[1:experts].reshape((experts - 1) * capacity, width_ff)], axis=0
        )
        turned = jnp.dot(value, basis_h[:, left:right], preferred_element_type=f32).astype(bf16)
        h_ref[:, left:right] = turned
        square = jnp.square(turned.astype(f32)).astype(bf16)
        hsq[:, left:right] = square
        return jnp.sum(square.astype(f32), axis=1, keepdims=True)

    row_h = [rotate_hidden(0, WIDE)]

    def core_copy(c):
        return pltpu.make_async_remote_copy(
            part.at[c, 1 - k],
            nearby.at[c],
            core_s.at[c],
            core_r.at[c],
            device_id={"dp_2": 1 - k},
            device_id_type=MESH,
        )

    def rs_copy(c, d):
        to = lax.rem(xz + d, chips)
        return pltpu.make_async_remote_copy(
            summed.at[c, to],
            far.at[c, d],
            rs_s.at[c, d],
            rs_r.at[c, d],
            device_id=chip_id(to),
            device_id_type=MESH,
        )

    def ag_copy(c, d):
        to = lax.rem(xz + d, chips)
        return pltpu.make_async_remote_copy(
            inv.at[c, k, xz],
            inv.at[c, k, xz],
            ag_s.at[c, d],
            ag_r.at[c, d],
            device_id=chip_id(to),
            device_id_type=MESH,
        )

    def ag_arrival(c, d):
        origin = lax.rem(xz + chips - d, chips)
        return pltpu.make_async_remote_copy(
            inv.at[c, k, origin],
            inv.at[c, k, origin],
            ag_s.at[c, d],
            ag_r.at[c, d],
            device_id=chip_id(origin),
            device_id_type=MESH,
        )

    def cg_copy(c, side):
        return pltpu.make_async_remote_copy(
            inv.at[c, side],
            inv.at[c, side],
            cg_s.at[c],
            cg_r.at[c],
            device_id={"dp_2": 1 - k},
            device_id_type=MESH,
        )

    def small_copy(d, slot):
        return pltpu.make_async_remote_copy(
            sums.at[me],
            sums.at[slot],
            small_s.at[d],
            small_r.at[d],
            device_id=dp_id(lax.rem(me + d, 2 * chips)),
            device_id_type=MESH,
        )

    def spread(pair):
        both = lax.dot_general(
            gsq[...],
            hsq[:, pair * WIDE : (pair + 1) * WIDE],
            (((0,), (0,)), ((), ())),
            preferred_element_type=f32,
        ).astype(bf16)
        for half in range(2):
            for q in range(2 * chips):
                first = q * 128 + half * half_rows
                part[2 * pair + half, q % 2, q // 2] = both[first : first + half_rows, :]
            core_copy(2 * pair + half).start()

    def share():
        own_sum = jnp.sum(
            jnp.concatenate(row_g, axis=0) * (row_h[0] + row_h[1]), axis=0, keepdims=True
        )
        sums[me] = jnp.broadcast_to(own_sum, (8, 128))
        each(1, 2 * chips, lambda d: small_copy(d, me).start())

    def stage_one(c):
        core_copy(c).wait()
        summed[c] = (part[c, k].astype(f32) + nearby[c].astype(f32)).astype(bf16)
        each(1, chips, lambda d: rs_copy(c, d).start())

    def stage_two(c, level):
        each(1, chips, lambda d: rs_copy(c, d).wait_recv())
        total = summed[c, xz].astype(f32)
        for d in range(1, chips):
            total = total + far[c, d].astype(f32)
        block = total * scale
        first, left = (c % 2) * half_rows, (c // 2) * WIDE
        corr[first : first + half_rows, left : left + WIDE] = block
        inv[c, k, xz] = (1.0 / (block + level)).astype(bf16)
        each(1, chips, lambda d: ag_copy(c, d).start())

    def stage_three(c):
        each(1, chips, lambda d: ag_arrival(c, d).wait_recv())
        cg_copy(c, k).start()

    def ready(c):
        cg_copy(c, 1 - k).wait_recv()

    lane = lax.broadcasted_iota(jnp.int32, acc.shape, 1)
    group = 4

    def score(unit, first, last):
        left = (unit // 2) * WIDE

        def step(t, _):
            parts = []
            for j in range(group):
                pieces = []
                for tile in range(chips):
                    row = (unit % 2) * chips + tile
                    pieces.append(
                        ordered[unit % 2, :, tile * 128 : (tile + 1) * 128]
                        * small[j % 2, t, j // 2, row : row + 1, :].astype(bf16)
                    )
                parts.append(jnp.concatenate(pieces, axis=1))
            scaled = jnp.concatenate(parts, axis=0)
            weights = inv[unit].reshape(width_d // 2, WIDE)
            product = jnp.dot(scaled, weights, preferred_element_type=f32)
            total = acc[...]
            for j in range(group):
                n = t * group + j
                value = None
                for side in range(WIDE // 128):
                    c = left // 128 + side
                    term = product[
                        j * rows : (j + 1) * rows, side * 128 : (side + 1) * 128
                    ] * (
                        h_ref[:, c * 128 : (c + 1) * 128].astype(f32)
                        * small[j % 2, t, j // 2, 16 + c : 17 + c, :]
                    )
                    value = term if value is None else value + term
                total = total + jnp.where(
                    lane == n, jnp.sum(value, axis=1, keepdims=True), 0.0
                )
            acc[...] = total
            return 0

        lax.fori_loop(first + z // 2, last + z // 2, step, 0)

    def small_arrival(d):
        small_copy(d, lax.rem(me + 2 * chips - d, 2 * chips)).wait_recv()

    spread(0)
    row_h.append(rotate_hidden(WIDE, width_ff))
    share()
    stage_one(0)
    stage_one(1)
    spread(1)
    spread(2)
    for half in range(2):
        for tile in range(chips):
            ordered[half, :, tile * 128 : (tile + 1) * 128] = halves(g_ref, half, tile)
    each(1, 2 * chips, small_arrival)
    complete = sums[0, 0:1, :]
    for n in range(1, 2 * chips):
        complete = complete + sums[n, 0:1, :]
    level = damp_ref[0] * (complete * (scale / (width_d * width_ff)) + eps)
    level = jnp.concatenate([level] * (WIDE // 128), axis=1)

    ask_core(1 - k).wait_recv()
    stages = {"A": stage_one, "C": lambda c: stage_two(c, level), "E": stage_three, "R": ready}
    for act, c, *span in ORDER:
        if act == "S":
            score(c, *span)
        else:
            stages[act](c)

    turned_scores = (acc[...] / root).T[: ret_out.shape[1], :]
    blank = jnp.zeros((ret_out.shape[1], 128 - capacity), f32)
    for d in range(experts):
        ret_out[d] = jnp.concatenate(
            [turned_scores[:, d * capacity : (d + 1) * capacity], blank], axis=1
        )

    def ret_copy(d, slot):
        return pltpu.make_async_remote_copy(
            ret_out.at[d],
            ret_in.at[slot],
            ret_s.at[d],
            ret_r.at[d],
            device_id={"expert": lax.rem(e + experts - d, experts)},
            device_id_type=MESH,
        )

    each(1, experts, lambda d: ret_copy(d, e).start())
    leave = pltpu.make_async_copy(corr, corr_ref, basis_sem.at[6])
    leave.start()
    ret_in[e] = ret_out[0]
    for c in range(chunks):
        each(1, chips, lambda d: rs_copy(c, d).wait_send())
        each(1, chips, lambda d: ag_copy(c, d).wait_send())
        cg_copy(c, k).wait_send()
    each(1, 2 * chips, lambda d: small_copy(d, me).wait_send())
    ask_near(z).wait_send()
    each(1, 4, lambda d: ask_line(d, x).wait_send())
    ask_core(k).wait_send()
    each(1, experts, lambda d: dg_copy(d).wait_send())
    each(1, experts, lambda d: dh_copy(d).wait_send())
    each(1, experts, lambda d: ret_copy(d, lax.rem(e + d, experts)).wait_recv())
    arrived = jnp.concatenate([ret_in[j] for j in range(experts)], axis=1)
    high = arrived.astype(bf16)
    rest = arrived - high.astype(f32)
    middle = rest.astype(bf16)
    low = (rest - middle.astype(f32)).astype(bf16)
    result = jnp.dot(
        jnp.concatenate([high, middle, low], axis=0),
        back[...].reshape(experts * 128, sent),
        preferred_element_type=f32,
    )
    queries = ret_out.shape[1]
    result = result[:queries] + result[queries : 2 * queries] + result[2 * queries :]
    for j in range(top):
        out_ref[j] = result[:, j * tokens : (j + 1) * tokens]
    each(1, experts, lambda d: ret_copy(d, e).wait_send())
    leave.wait()


def write_kernel(picked_ref, sums_ref, scores_ref, corr_ref, picked, sums, sems):
    pieces = 4
    tall = sums.shape[0] // pieces
    cuts = [pl.ds(i * tall, tall) for i in range(pieces)]
    pairs = [(sums_ref.at[cut], sums.at[cut], corr_ref.at[cut]) for cut in cuts]
    pairs.append((picked_ref, picked, scores_ref))
    taken = [
        pltpu.make_async_copy(source, held, sems.at[0, i])
        for i, (source, held, _) in enumerate(pairs)
    ]
    put = [
        pltpu.make_async_copy(held, target, sems.at[1, i])
        for i, (_, held, target) in enumerate(pairs)
    ]
    for copy in taken:
        copy.start()
    for first, second in zip(taken, put):
        first.wait()
        second.start()
    for copy in put:
        copy.wait()


def body(
    token_hidden,
    token_grad,
    routes,
    route_weight,
    gradient_eigenbasis,
    basis_hidden,
    query_hidden,
    query_grad,
    query_ids,
    damping,
):
    experts = lax.axis_size("expert")
    replicas = lax.axis_size(DP)
    tokens, top, width_ff = token_hidden.shape
    width_d = token_grad.shape[1]
    capacity = tokens * top * 3 // (2 * experts)
    rows = experts * capacity
    chips = replicas // 2
    chunks = 2 * width_ff // WIDE
    bf16, f32 = jnp.bfloat16, jnp.float32
    block = width_d // replicas
    dma = pltpu.SemaphoreType.DMA
    vmem = pl.BlockSpec(memory_space=pltpu.VMEM)
    anywhere = pl.BlockSpec(memory_space=pl.ANY)
    smem = pl.BlockSpec(memory_space=pltpu.SMEM)
    picked, corrections = pl.pallas_call(
        functools.partial(
            back_kernel, 1.0 / (replicas * experts * capacity), math.sqrt(width_d * width_ff)
        ),
        out_shape=(
            jax.ShapeDtypeStruct((top, replicas, tokens), f32),
            jax.ShapeDtypeStruct((block, width_ff), f32),
        ),
        in_specs=[vmem] * 2 + [anywhere] * 6 + [smem] * 2,
        out_specs=(vmem, anywhere),
        scratch_shapes=[
            pltpu.VMEM((width_d, width_d), bf16),
            pltpu.VMEM((width_ff, width_ff), bf16),
            pltpu.VMEM(token_hidden.shape, bf16),
            pltpu.VMEM(token_grad.shape, bf16),
            pltpu.VMEM(query_grad.shape[1:], bf16),
            pltpu.VMEM(query_hidden.shape[1:], bf16),
            pltpu.VMEM((experts, capacity, width_d), bf16),
            pltpu.VMEM((experts, capacity, width_ff), bf16),
            pltpu.VMEM((experts, capacity, width_d), bf16),
            pltpu.VMEM((experts, capacity, width_ff), bf16),
            pltpu.VMEM((rows, width_d), bf16),
            pltpu.VMEM((rows, width_ff), bf16),
            pltpu.VMEM((rows, width_d), bf16),
            pltpu.VMEM((rows, width_ff), bf16),
            pltpu.VMEM((2, chips // 2, 2, 24, 128), f32),
            pltpu.VMEM((replicas, 8, 128), f32),
            pltpu.VMEM((block, width_ff), f32),
            pltpu.VMEM((2, rows, width_d // 2), bf16),
            pltpu.VMEM((experts, 128, tokens * top), bf16),
            pltpu.VMEM((chunks, 2, chips, block // 2, WIDE), bf16),
            pltpu.VMEM((chunks, chips, block // 2, WIDE), bf16),
            pltpu.VMEM((chunks, chips, block // 2, WIDE), bf16),
            pltpu.VMEM((chunks, chips, block // 2, WIDE), bf16),
            pltpu.VMEM((chunks, 2, chips, block // 2, WIDE), bf16),
            pltpu.VMEM((rows, 128), f32),
            pltpu.VMEM((experts, replicas, 128), f32),
            pltpu.VMEM((experts, replicas, 128), f32),
            dma((7,)),
            dma((experts,)),
            dma((experts,)),
            dma((experts,)),
            dma((experts,)),
            dma((replicas,)),
            dma((replicas,)),
            dma((5,)),
            dma((5,)),
            dma((chunks,)),
            dma((chunks,)),
            dma((chunks, chips)),
            dma((chunks, chips)),
            dma((chunks, chips)),
            dma((chunks, chips)),
            dma((chunks,)),
            dma((chunks,)),
            dma((experts,)),
            dma((experts,)),
        ],
        compiler_params=pltpu.CompilerParams(
            collective_id=0, has_side_effects=True, vmem_limit_bytes=60 * 1024 * 1024
        ),
    )(
        routes.T,
        route_weight.T,
        token_hidden,
        token_grad,
        gradient_eigenbasis[0],
        basis_hidden[0],
        query_grad[0],
        query_hidden[0],
        query_ids,
        damping,
    )
    picked, corrections = pl.pallas_call(
        write_kernel,
        out_shape=tuple(jax.ShapeDtypeStruct(a.shape, f32) for a in (picked, corrections)),
        in_specs=[anywhere] * 2,
        out_specs=(anywhere, anywhere),
        scratch_shapes=[
            pltpu.VMEM(picked.shape, f32),
            pltpu.VMEM(corrections.shape, f32),
            dma((2, 5)),
        ],
        compiler_params=pltpu.CompilerParams(vmem_limit_bytes=60 * 1024 * 1024),
    )(picked, corrections)
    return (picked.transpose(2, 0, 1), corrections[None])


def solution(mesh):
    torus = Mesh(
        mesh.devices.reshape(mesh.shape["expert"], 4, 2, 2), ("expert", "dp_0", "dp_1", "dp_2")
    )
    placed = (
        P(EXPERT_DP, None, None),
        P(EXPERT_DP, None),
        P(EXPERT_DP, None),
        P(EXPERT_DP, None),
        P("expert", None, None),
        P("expert", None, None),
        P("expert", DP, None),
        P("expert", DP, None),
        P("expert", DP),
        P("expert"),
    )
    return jax.shard_map(
        body,
        mesh=torus,
        in_specs=placed,
        out_specs=(P(EXPERT_DP, None, None), P("expert", DP, None)),
        check_vma=False,
    )
```

```python
import functools
import math

import jax
import jax.numpy as jnp
from jax import lax
from jax.experimental import pallas as pl
from jax.experimental.pallas import tpu as pltpu
from jax.sharding import Mesh
from jax.sharding import PartitionSpec as P

DP = ("dp_0", "dp_1", "dp_2")
EXPERT_DP = ("expert", "dp_0", "dp_1", "dp_2")

eps = 1e-06


MESH = pl.DeviceIdType.MESH
WIDE = 256
ORDER = (
    ("C", 0), ("A", 2), ("C", 1), ("A", 3), ("E", 0), ("R", 0), ("S", 0, 0, 1), ("C", 2), ("A", 4),
    ("S", 0, 1, 3), ("E", 1), ("S", 0, 3, 4), ("R", 1), ("S", 1, 0, 1), ("C", 3), ("A", 5),
    ("S", 1, 1, 3), ("E", 2), ("S", 1, 3, 4), ("R", 2), ("S", 2, 0, 1), ("C", 4), ("S", 2, 1, 3),
    ("E", 3), ("S", 2, 3, 4), ("R", 3), ("S", 3, 0, 1), ("C", 5), ("S", 3, 1, 3), ("E", 4),
    ("S", 3, 3, 4), ("R", 4), ("S", 4, 0, 2), ("E", 5), ("S", 4, 2, 4), ("R", 5), ("S", 5, 0, 4),
)


def pair_of(tile, chips):
    return tuple((q % chips) * 2 + q // chips for q in (2 * tile, 2 * tile + 1))


def back_kernel(
    scale,
    root,
    routes_ref,
    weight_ref,
    hidden_ref,
    grad_ref,
    basis_g_ref,
    basis_h_ref,
    query_g_ref,
    query_h_ref,
    ids_ref,
    damp_ref,
    out_ref,
    corr_ref,
    basis_g,
    basis_h,
    token_hidden,
    token_grad,
    query_rows_g,
    query_rows_h,
    send_g,
    send_h,
    held_g,
    held_h,
    g_ref,
    h_ref,
    gsq,
    hsq,
    small,
    sums,
    corr,
    ordered,
    back,
    part,
    nearby,
    summed,
    far,
    inv,
    acc,
    ret_out,
    ret_in,
    basis_sem,
    dg_s,
    dg_r,
    dh_s,
    dh_r,
    small_s,
    small_r,
    ask_s,
    ask_r,
    core_s,
    core_r,
    rs_s,
    rs_r,
    ag_s,
    ag_r,
    cg_s,
    cg_r,
    ret_s,
    ret_r,
):
    e = lax.axis_index("expert")
    x = lax.axis_index("dp_0")
    z = lax.axis_index("dp_1")
    k = lax.axis_index("dp_2")
    xz = x * 2 + z
    chips = part.shape[2]
    experts = ret_out.shape[0]
    capacity = held_g.shape[1]
    rows, width_d = g_ref.shape
    width_ff = h_ref.shape[1]
    chunks = part.shape[0]
    half_rows = part.shape[3]
    bf16, f32 = jnp.bfloat16, jnp.float32

    def halves(row, unit_half, tile):
        return jnp.concatenate(
            [
                row[:, d * 128 + unit_half * half_rows : d * 128 + (unit_half + 1) * half_rows]
                for d in pair_of(tile, chips)
            ],
            axis=1,
        )

    def dp_id(index):
        return {"dp_0": index // 4, "dp_1": lax.rem(index // 2, 2), "dp_2": lax.rem(index, 2)}

    def chip_id(index):
        return {"dp_0": index // 2, "dp_1": lax.rem(index, 2)}

    me = xz * 2 + k
    barrier = pltpu.get_barrier_semaphore()

    def greet_dp(d, _):
        pl.semaphore_signal(
            barrier, 1, device_id=dp_id(lax.rem(me + d, 2 * chips)), device_id_type=MESH
        )
        return 0

    def greet_expert(d, _):
        pl.semaphore_signal(
            barrier, 1, device_id={"expert": lax.rem(e + d, experts)}, device_id_type=MESH
        )
        return 0

    lax.fori_loop(1, 2 * chips, greet_dp, 0)
    lax.fori_loop(1, experts, greet_expert, 0)
    loads = [
        pltpu.make_async_copy(source, target, basis_sem.at[index])
        for index, (source, target) in enumerate(
            (
                (grad_ref, token_grad),
                (hidden_ref, token_hidden),
                (query_g_ref, query_rows_g),
                (query_h_ref, query_rows_h),
                (basis_h_ref, basis_h),
                (basis_g_ref, basis_g),
            )
        )
    ]
    for load in loads:
        load.start()

    def each(first, last, act):
        def once(d, _):
            act(d)
            return 0

        lax.fori_loop(first, last, once, 0)

    tokens = grad_ref.shape[0]
    top = routes_ref.shape[0]
    sent = tokens * top
    named = jnp.concatenate([routes_ref[j : j + 1, :] for j in range(top)], axis=1)
    onehot = (named == lax.broadcasted_iota(jnp.int32, (16, sent), 0)).astype(f32)

    def order_of(axis):
        index = lax.broadcasted_iota(jnp.int32, (sent, sent), axis)
        return jnp.where(index < tokens, index * top, (index - tokens) * top + 1)

    earlier = (order_of(0) < order_of(1)).astype(f32).astype(bf16)
    before = jnp.dot(onehot.astype(bf16), earlier, preferred_element_type=f32)
    within = jnp.sum(before * onehot, axis=0, keepdims=True).astype(jnp.int32)
    slots = named * capacity + within
    chosen = (slots == lax.broadcasted_iota(jnp.int32, (experts * capacity, sent), 0)).astype(f32)
    weights = jnp.concatenate([weight_ref[j : j + 1, :] for j in range(top)], axis=1)
    weight = jnp.sum(chosen * weights, axis=1, keepdims=True)
    picks = [chosen[:, j * tokens : (j + 1) * tokens].astype(bf16) for j in range(top)]
    loads[0].wait()
    gathered = jnp.dot(sum(picks[1:], picks[0]), token_grad[...], preferred_element_type=f32)
    send_g[...] = (weight * gathered).astype(bf16).reshape(send_g.shape)

    def dispatch_copy(source, target, ssem, rsem, d):
        to = lax.rem(e + d, experts)
        return pltpu.make_async_remote_copy(
            source.at[to],
            target.at[d],
            ssem.at[d],
            rsem.at[d],
            device_id={"expert": to},
            device_id_type=MESH,
        )

    def dg_copy(d):
        return dispatch_copy(send_g, held_g, dg_s, dg_r, d)

    def dh_copy(d):
        return dispatch_copy(send_h, held_h, dh_s, dh_r, d)

    pl.semaphore_wait(barrier, 2 * chips - 1 + experts - 1)
    each(1, experts, lambda d: dg_copy(d).start())
    loads[1].wait()
    hidden = token_hidden[...].astype(f32)
    moved = None
    for j in range(top):
        part_j = jnp.dot(picks[j], hidden[:, j, :].astype(bf16), preferred_element_type=f32)
        moved = part_j if moved is None else moved + part_j
    send_h[...] = moved.astype(bf16).reshape(send_h.shape)
    each(1, experts, lambda d: dh_copy(d).start())
    acc[...] = jnp.zeros_like(acc)
    back[...] = jnp.zeros_like(back)
    for j in range(experts):
        back[j, :capacity, :] = chosen[j * capacity : (j + 1) * capacity].astype(bf16)

    def rotate(value, basis, rotated, squared, first):
        turned = jnp.dot(value, basis[...], preferred_element_type=f32).astype(bf16)
        count = value.shape[0]
        rotated[first : first + count, :] = turned
        square = jnp.square(turned.astype(f32)).astype(bf16)
        squared[first : first + count, :] = square
        return jnp.sum(square.astype(f32), axis=1, keepdims=True)

    for load in loads[2:]:
        load.wait()
    row_g = [rotate(send_g[e], basis_g, g_ref, gsq, 0)]
    query_row = lax.broadcasted_iota(jnp.int32, (query_g_ref.shape[0], 1), 0) == ids_ref[0, 0]

    def query(ref, basis):
        turned = jnp.dot(ref[...], basis[...], preferred_element_type=f32)
        one = jnp.sum(jnp.where(query_row, turned, 0.0), axis=0, keepdims=True)
        return one.astype(bf16).astype(f32)

    query_g = query(query_rows_g, basis_g)
    query_h = query(query_rows_h, basis_h)
    for j in range(width_d // 128):
        small[k, x, z, j : j + 1, :] = halves(query_g, j // chips, j % chips)
    for j in range(width_ff // 128):
        small[k, x, z, 16 + j : 17 + j, :] = query_h[:, j * 128 : (j + 1) * 128]

    def ask_near(half):
        return pltpu.make_async_remote_copy(
            small.at[k, x, half],
            small.at[k, x, half],
            ask_s.at[0],
            ask_r.at[0],
            device_id={"dp_1": 1 - z},
            device_id_type=MESH,
        )

    def ask_line(d, line):
        return pltpu.make_async_remote_copy(
            small.at[k, line],
            small.at[k, line],
            ask_s.at[d],
            ask_r.at[d],
            device_id={"dp_0": lax.rem(x + d, 4)},
            device_id_type=MESH,
        )

    def ask_core(side):
        return pltpu.make_async_remote_copy(
            small.at[side],
            small.at[side],
            ask_s.at[4],
            ask_r.at[4],
            device_id={"dp_2": 1 - k},
            device_id_type=MESH,
        )

    ask_near(z).start()
    for first, last in ((1, experts // 2), (experts // 2, experts)):
        each(first, last, lambda d: dg_copy(d).wait_recv())
        row_g.append(
            rotate(
                held_g[first:last].reshape((last - first) * capacity, width_d),
                basis_g,
                g_ref,
                gsq,
                first * capacity,
            )
        )
        if first == 1:
            ask_near(1 - z).wait_recv()
            each(1, 4, lambda d: ask_line(d, x).start())
        else:
            each(1, 4, lambda d: ask_line(d, lax.rem(x + 4 - d, 4)).wait_recv())
            ask_core(k).start()
    each(1, experts, lambda d: dh_copy(d).wait_recv())
    row_h = rotate(
        jnp.concatenate(
            [send_h[e], held_h[1:experts].reshape((experts - 1) * capacity, width_ff)], axis=0
        ),
        basis_h,
        h_ref,
        hsq,
        0,
    )

    def core_copy(c):
        return pltpu.make_async_remote_copy(
            part.at[c, 1 - k],
            nearby.at[c],
            core_s.at[c],
            core_r.at[c],
            device_id={"dp_2": 1 - k},
            device_id_type=MESH,
        )

    def rs_copy(c, d):
        to = lax.rem(xz + d, chips)
        return pltpu.make_async_remote_copy(
            summed.at[c, to],
            far.at[c, d],
            rs_s.at[c, d],
            rs_r.at[c, d],
            device_id=chip_id(to),
            device_id_type=MESH,
        )

    def ag_copy(c, d):
        to = lax.rem(xz + d, chips)
        return pltpu.make_async_remote_copy(
            inv.at[c, k, xz],
            inv.at[c, k, xz],
            ag_s.at[c, d],
            ag_r.at[c, d],
            device_id=chip_id(to),
            device_id_type=MESH,
        )

    def ag_arrival(c, d):
        origin = lax.rem(xz + chips - d, chips)
        return pltpu.make_async_remote_copy(
            inv.at[c, k, origin],
            inv.at[c, k, origin],
            ag_s.at[c, d],
            ag_r.at[c, d],
            device_id=chip_id(origin),
            device_id_type=MESH,
        )

    def cg_copy(c, side):
        return pltpu.make_async_remote_copy(
            inv.at[c, side],
            inv.at[c, side],
            cg_s.at[c],
            cg_r.at[c],
            device_id={"dp_2": 1 - k},
            device_id_type=MESH,
        )

    def small_copy(d, slot):
        return pltpu.make_async_remote_copy(
            sums.at[me],
            sums.at[slot],
            small_s.at[d],
            small_r.at[d],
            device_id=dp_id(lax.rem(me + d, 2 * chips)),
            device_id_type=MESH,
        )

    def spread(pair):
        both = lax.dot_general(
            gsq[...],
            hsq[:, pair * WIDE : (pair + 1) * WIDE],
            (((0,), (0,)), ((), ())),
            preferred_element_type=f32,
        ).astype(bf16)
        for half in range(2):
            for q in range(2 * chips):
                first = q * 128 + half * half_rows
                part[2 * pair + half, q % 2, q // 2] = both[first : first + half_rows, :]
            core_copy(2 * pair + half).start()

    def share():
        own_sum = jnp.sum(jnp.concatenate(row_g, axis=0) * row_h, axis=0, keepdims=True)
        sums[me] = jnp.broadcast_to(own_sum, (8, 128))
        each(1, 2 * chips, lambda d: small_copy(d, me).start())

    def stage_one(c):
        core_copy(c).wait()
        summed[c] = (part[c, k].astype(f32) + nearby[c].astype(f32)).astype(bf16)
        each(1, chips, lambda d: rs_copy(c, d).start())

    def stage_two(c, level):
        each(1, chips, lambda d: rs_copy(c, d).wait_recv())
        total = summed[c, xz].astype(f32)
        for d in range(1, chips):
            total = total + far[c, d].astype(f32)
        block = total * scale
        first, left = (c % 2) * half_rows, (c // 2) * WIDE
        corr[first : first + half_rows, left : left + WIDE] = block
        inv[c, k, xz] = (1.0 / (block + level)).astype(bf16)
        each(1, chips, lambda d: ag_copy(c, d).start())

    def stage_three(c):
        each(1, chips, lambda d: ag_arrival(c, d).wait_recv())
        cg_copy(c, k).start()

    def ready(c):
        cg_copy(c, 1 - k).wait_recv()

    lane = lax.broadcasted_iota(jnp.int32, acc.shape, 1)
    group = 4

    def score(unit, first, last):
        left = (unit // 2) * WIDE

        def step(t, _):
            parts = []
            for j in range(group):
                pieces = []
                for tile in range(chips):
                    row = (unit % 2) * chips + tile
                    pieces.append(
                        ordered[unit % 2, :, tile * 128 : (tile + 1) * 128]
                        * small[j % 2, t, j // 2, row : row + 1, :].astype(bf16)
                    )
                parts.append(jnp.concatenate(pieces, axis=1))
            scaled = jnp.concatenate(parts, axis=0)
            weights = inv[unit].reshape(width_d // 2, WIDE)
            product = jnp.dot(scaled, weights, preferred_element_type=f32)
            total = acc[...]
            for j in range(group):
                n = t * group + j
                value = None
                for side in range(WIDE // 128):
                    c = left // 128 + side
                    term = product[
                        j * rows : (j + 1) * rows, side * 128 : (side + 1) * 128
                    ] * (
                        h_ref[:, c * 128 : (c + 1) * 128].astype(f32)
                        * small[j % 2, t, j // 2, 16 + c : 17 + c, :]
                    )
                    value = term if value is None else value + term
                total = total + jnp.where(
                    lane == n, jnp.sum(value, axis=1, keepdims=True), 0.0
                )
            acc[...] = total
            return 0

        lax.fori_loop(first + z // 2, last + z // 2, step, 0)

    def small_arrival(d):
        small_copy(d, lax.rem(me + 2 * chips - d, 2 * chips)).wait_recv()

    spread(0)
    share()
    spread(1)
    stage_one(0)
    stage_one(1)
    spread(2)
    for half in range(2):
        for tile in range(chips):
            ordered[half, :, tile * 128 : (tile + 1) * 128] = halves(g_ref, half, tile)
    each(1, 2 * chips, small_arrival)
    complete = sums[0, 0:1, :]
    for n in range(1, 2 * chips):
        complete = complete + sums[n, 0:1, :]
    level = damp_ref[0] * (complete * (scale / (width_d * width_ff)) + eps)
    level = jnp.concatenate([level] * (WIDE // 128), axis=1)

    ask_core(1 - k).wait_recv()
    stages = {"A": stage_one, "C": lambda c: stage_two(c, level), "E": stage_three, "R": ready}
    for act, c, *span in ORDER:
        if act == "S":
            score(c, *span)
        else:
            stages[act](c)

    turned_scores = (acc[...] / root).T[: ret_out.shape[1], :]
    blank = jnp.zeros((ret_out.shape[1], 128 - capacity), f32)
    for d in range(experts):
        ret_out[d] = jnp.concatenate(
            [turned_scores[:, d * capacity : (d + 1) * capacity], blank], axis=1
        )

    def ret_copy(d, slot):
        return pltpu.make_async_remote_copy(
            ret_out.at[d],
            ret_in.at[slot],
            ret_s.at[d],
            ret_r.at[d],
            device_id={"expert": lax.rem(e + experts - d, experts)},
            device_id_type=MESH,
        )

    each(1, experts, lambda d: ret_copy(d, e).start())
    leave = pltpu.make_async_copy(corr, corr_ref, basis_sem.at[6])
    leave.start()
    ret_in[e] = ret_out[0]
    for c in range(chunks):
        each(1, chips, lambda d: rs_copy(c, d).wait_send())
        each(1, chips, lambda d: ag_copy(c, d).wait_send())
        cg_copy(c, k).wait_send()
    each(1, 2 * chips, lambda d: small_copy(d, me).wait_send())
    ask_near(z).wait_send()
    each(1, 4, lambda d: ask_line(d, x).wait_send())
    ask_core(k).wait_send()
    each(1, experts, lambda d: dg_copy(d).wait_send())
    each(1, experts, lambda d: dh_copy(d).wait_send())
    each(1, experts, lambda d: ret_copy(d, lax.rem(e + d, experts)).wait_recv())
    arrived = jnp.concatenate([ret_in[j] for j in range(experts)], axis=1)
    high = arrived.astype(bf16)
    rest = arrived - high.astype(f32)
    middle = rest.astype(bf16)
    low = (rest - middle.astype(f32)).astype(bf16)
    result = jnp.dot(
        jnp.concatenate([high, middle, low], axis=0),
        back[...].reshape(experts * 128, sent),
        preferred_element_type=f32,
    )
    queries = ret_out.shape[1]
    result = result[:queries] + result[queries : 2 * queries] + result[2 * queries :]
    for j in range(top):
        out_ref[j] = result[:, j * tokens : (j + 1) * tokens]
    each(1, experts, lambda d: ret_copy(d, e).wait_send())
    leave.wait()


def write_kernel(picked_ref, sums_ref, scores_ref, corr_ref, picked, sums, sems):
    pairs = ((sums_ref, sums, corr_ref), (picked_ref, picked, scores_ref))
    taken = [
        pltpu.make_async_copy(source, held, sems.at[0, i])
        for i, (source, held, _) in enumerate(pairs)
    ]
    put = [
        pltpu.make_async_copy(held, target, sems.at[1, i])
        for i, (_, held, target) in enumerate(pairs)
    ]
    for copy in taken:
        copy.start()
    for first, second in zip(taken, put):
        first.wait()
        second.start()
    for copy in put:
        copy.wait()


def body(
    token_hidden,
    token_grad,
    routes,
    route_weight,
    gradient_eigenbasis,
    basis_hidden,
    query_hidden,
    query_grad,
    query_ids,
    damping,
):
    experts = lax.axis_size("expert")
    replicas = lax.axis_size(DP)
    tokens, top, width_ff = token_hidden.shape
    width_d = token_grad.shape[1]
    capacity = tokens * top * 3 // (2 * experts)
    rows = experts * capacity
    chips = replicas // 2
    chunks = 2 * width_ff // WIDE
    bf16, f32 = jnp.bfloat16, jnp.float32
    block = width_d // replicas
    dma = pltpu.SemaphoreType.DMA
    vmem = pl.BlockSpec(memory_space=pltpu.VMEM)
    anywhere = pl.BlockSpec(memory_space=pl.ANY)
    smem = pl.BlockSpec(memory_space=pltpu.SMEM)
    picked, corrections = pl.pallas_call(
        functools.partial(
            back_kernel, 1.0 / (replicas * experts * capacity), math.sqrt(width_d * width_ff)
        ),
        out_shape=(
            jax.ShapeDtypeStruct((top, replicas, tokens), f32),
            jax.ShapeDtypeStruct((block, width_ff), f32),
        ),
        in_specs=[vmem] * 2 + [anywhere] * 6 + [smem] * 2,
        out_specs=(vmem, anywhere),
        scratch_shapes=[
            pltpu.VMEM((width_d, width_d), bf16),
            pltpu.VMEM((width_ff, width_ff), bf16),
            pltpu.VMEM(token_hidden.shape, bf16),
            pltpu.VMEM(token_grad.shape, bf16),
            pltpu.VMEM(query_grad.shape[1:], bf16),
            pltpu.VMEM(query_hidden.shape[1:], bf16),
            pltpu.VMEM((experts, capacity, width_d), bf16),
            pltpu.VMEM((experts, capacity, width_ff), bf16),
            pltpu.VMEM((experts, capacity, width_d), bf16),
            pltpu.VMEM((experts, capacity, width_ff), bf16),
            pltpu.VMEM((rows, width_d), bf16),
            pltpu.VMEM((rows, width_ff), bf16),
            pltpu.VMEM((rows, width_d), bf16),
            pltpu.VMEM((rows, width_ff), bf16),
            pltpu.VMEM((2, chips // 2, 2, 24, 128), f32),
            pltpu.VMEM((replicas, 8, 128), f32),
            pltpu.VMEM((block, width_ff), f32),
            pltpu.VMEM((2, rows, width_d // 2), bf16),
            pltpu.VMEM((experts, 128, tokens * top), bf16),
            pltpu.VMEM((chunks, 2, chips, block // 2, WIDE), bf16),
            pltpu.VMEM((chunks, chips, block // 2, WIDE), bf16),
            pltpu.VMEM((chunks, chips, block // 2, WIDE), bf16),
            pltpu.VMEM((chunks, chips, block // 2, WIDE), bf16),
            pltpu.VMEM((chunks, 2, chips, block // 2, WIDE), bf16),
            pltpu.VMEM((rows, 128), f32),
            pltpu.VMEM((experts, replicas, 128), f32),
            pltpu.VMEM((experts, replicas, 128), f32),
            dma((7,)),
            dma((experts,)),
            dma((experts,)),
            dma((experts,)),
            dma((experts,)),
            dma((replicas,)),
            dma((replicas,)),
            dma((5,)),
            dma((5,)),
            dma((chunks,)),
            dma((chunks,)),
            dma((chunks, chips)),
            dma((chunks, chips)),
            dma((chunks, chips)),
            dma((chunks, chips)),
            dma((chunks,)),
            dma((chunks,)),
            dma((experts,)),
            dma((experts,)),
        ],
        compiler_params=pltpu.CompilerParams(
            collective_id=0, has_side_effects=True, vmem_limit_bytes=60 * 1024 * 1024
        ),
    )(
        routes.T,
        route_weight.T,
        token_hidden,
        token_grad,
        gradient_eigenbasis[0],
        basis_hidden[0],
        query_grad[0],
        query_hidden[0],
        query_ids,
        damping,
    )
    picked, corrections = pl.pallas_call(
        write_kernel,
        out_shape=tuple(jax.ShapeDtypeStruct(a.shape, f32) for a in (picked, corrections)),
        in_specs=[anywhere] * 2,
        out_specs=(anywhere, anywhere),
        scratch_shapes=[
            pltpu.VMEM(picked.shape, f32),
            pltpu.VMEM(corrections.shape, f32),
            dma((2, 2)),
        ],
        compiler_params=pltpu.CompilerParams(vmem_limit_bytes=60 * 1024 * 1024),
    )(picked, corrections)
    return (picked.transpose(2, 0, 1), corrections[None])


def solution(mesh):
    torus = Mesh(
        mesh.devices.reshape(mesh.shape["expert"], 4, 2, 2), ("expert", "dp_0", "dp_1", "dp_2")
    )
    placed = (
        P(EXPERT_DP, None, None),
        P(EXPERT_DP, None),
        P(EXPERT_DP, None),
        P(EXPERT_DP, None),
        P("expert", None, None),
        P("expert", None, None),
        P("expert", DP, None),
        P("expert", DP, None),
        P("expert", DP),
        P("expert"),
    )
    return jax.shard_map(
        body,
        mesh=torus,
        in_specs=placed,
        out_specs=(P(EXPERT_DP, None, None), P("expert", DP, None)),
        check_vma=False,
    )
```
